512 devices in a mesh: section: 2 (over core), dp: 64 (over z, y), mp: 4 (over x).
Axes of the slice: x: 4, y: 4, z: 16, core: 2. Of those that a mesh axis runs over, the one named last changes fastest.
Arguments:
- qkv: bfloat16 [8192, 3072], P('dp', ('section', 'mp')), may hold values from -6 to 6
- kv_cache: bfloat16 [4096, 8, 2048], P('dp', None, ('section', 'mp')), may hold values from -6 to 6
- residual: bfloat16 [8192, 2048], P('dp'), may hold values from -6 to 6
- out_weight: bfloat16 [1024, 2048], P(('section', 'mp')), may hold values from -0.1875 to 0.1875
- moe_gain: float32 [2048], replicated, may hold values from 0.1 to 1.9
- w_gate: bfloat16 [64, 2048, 1408], P('dp', None, ('section', 'mp')), may hold values from -0.125 to 0.125
- w_up: bfloat16 [64, 2048, 1408], P('dp', None, ('section', 'mp')), may hold values from -0.125 to 0.125
- w_down: bfloat16 [64, 1408, 2048], P('dp', ('section', 'mp')), may hold values from -0.15625 to 0.15625
- seg_ids: int32 [64, 1, 128], P('dp'), may hold values from 0 to 3, never falling along the last dimension, each value on 1 to 64 neighbouring positions
- prefix_blocks: int32 [64, 1, 4], P('dp'), may hold values from 1 to 32, 64 in all within a row
- owners: int32 [64, 1, 64, 1], replicated, may hold values from 0 to 63; in each aligned block of 64 rows (0 to 63, 64 to 127, ..., all dimensions but the last counted through in order) at most 3 rows name the same one
- slot_ids: int32 [64, 1, 64], replicated, may hold values from 0 to 63
- expert_ids: int32 [8192, 4], P('dp'), may hold values from 0 to 63, all different within a row; in each aligned block of 16 rows (0 to 15, 16 to 31, ...) at most 2 rows name the same one
- gate_weights: float32 [8192, 4], P('dp'), may hold values from 0.05 to 0.5
Outputs:
- layer_out: bfloat16 [8192, 2048], P('dp', ('section', 'mp'))
The draws below stay inside these ranges and needn't reach their ends.
Inputs may be any that keep to these rules, and one draw needn't show every extreme that they name: seg_ids[g, m] never falls along the tokens; each of the 4 requests has 1 to 64 tokens, one exactly 64. `prefix_blocks`: the 4 counts of each (g, m) sum to 64, one of them is 32. `owners`: in each block table of 64 entries no owner appears more than 3 times, and some owner appears exactly 3 times in some table. `expert_ids`: each token names 4 different experts; in each aligned block of 16 tokens no expert is named by more than 2 tokens, a bound that some block reaches.
All inputs are finite; a program needn't handle non-finite values.
Results may differ from the reference program's by a relative error of at most 0.009.
Values may be sent and summed in bfloat16 or wider, within the bound.
No kernel may reach another device: no remote copies, remote signals or barrier semaphores. Data moves between devices by JAX's collectives and lax.ppermute only.
A program may use at most 64 MiB of HBM per device.

```python
import math
from functools import partial
import jax
import jax.numpy as jnp
import numpy as np
from jax import lax

D = 2048
HEADS = 8
HEAD_DIM = 128
FFE = 1408
TOPK = 4
MICRO = 1
PREF = 64
BLK = 8
SLOTS = 64
SEGS = 4
SPLIT = 8
EXPERTS = 64
TOKENS = 8192
MB = 128
QROWS = 16
CAPQ = 2
OWN_CAP = 3
SEG_MOST = 64
PMOST = 32
N_DP = 64


def draw_qkv(key, part):
    shape = (TOKENS, HEADS, 3, HEAD_DIM)
    base = jnp.clip(jax.random.normal(key, shape, jnp.float32), -6.0, 6.0)
    return base.reshape(TOKENS, HEADS * 3 * HEAD_DIM).astype(jnp.bfloat16)


def set_ends(result, rng, low, top_value):
    spot = [jax.random.randint(jax.random.fold_in(rng, axis), (), 0, length) for axis, length in enumerate(result.shape)]
    longest = result.shape.index(max(result.shape))
    beside = spot[:longest] + [(spot[longest] + 1) % result.shape[longest]] + spot[longest + 1:]
    return result.at[tuple(spot)].set(low).at[tuple(beside)].set(top_value)


def block_levels(own_key, shape, shards, least, largest):
    loudness, own = 1.0, jax.random.fold_in(own_key, 6)
    for dim, shards_of in shards:
        heights = jnp.exp(jax.random.uniform(jax.random.fold_in(own, dim), (shards_of,), jnp.float32, least / len(shards), largest / len(shards)))
        loudness = loudness * jnp.repeat(heights, shape[dim] // shards_of).reshape([-1 if axis == dim else 1 for axis in range(len(shape))])
    return loudness


def profile(number_of, total, bound, slope):
    weights = [(1 << 20) // math.isqrt(grade ** slope) + 1 for grade in range(2, number_of + 1)]
    rest, holding = total - bound - (number_of - 1), [1] * (number_of - 1)
    while rest > 0:
        free = [i for i in range(number_of - 1) if holding[i] < bound]
        whole, left = sum([weights[i] for i in free]), rest
        for i in free:
            extra = min(bound - holding[i], max(1, left * weights[i] // whole), rest)
            holding[i] = holding[i] + extra
            rest = rest - extra
    return np.array([bound] + holding)


def uneven(own_key, amount, total, limit, lean):
    if amount == 2:
        one = jax.random.randint(own_key, (), max(1, total - limit), min(limit, total - 1) + 1)
        return jnp.stack([one, total - one])
    tallies = jnp.asarray(profile(amount, total, limit, lean), jnp.int32)
    couples = (amount - 1) // 2
    donor, receiver = tallies[1:1 + 2 * couples:2], tallies[2:2 + 2 * couples:2]
    margin = jnp.minimum(donor - 1, limit - receiver)
    moved = jax.random.randint(jax.random.fold_in(own_key, 1), (couples,), 0, 1 << 20) % (margin + 1)
    tallies = tallies.at[1:1 + 2 * couples:2].set(donor - moved).at[2:2 + 2 * couples:2].set(receiver + moved)
    return tallies[jax.random.permutation(jax.random.fold_in(own_key, 2), amount)]


def assign_block(own_key, own, number, rows, amount, top, bound, slope):
    order = jax.random.permutation(own_key, amount)
    heavy_load, usual = shares(amount, rows * top, bound, slope, True), shares(amount, rows * top, bound, slope, False)
    places = jnp.arange(amount)

    def named(sizes, offset_by):
        used = int((sizes > 0).sum())
        fixed = max(1, used // 4)
        passed = fixed + (places - fixed + offset_by * (used - fixed)) % max(1, amount - fixed)
        return jnp.zeros((amount,), jnp.int32).at[order[jnp.where(places < fixed, places, passed)]].set(jnp.asarray(sizes, jnp.int32))

    sizes = jnp.where(number % 4 == 0, named(heavy_load, number // 4), named(usual, number - number // 4 - 1))
    mixed = jax.random.permutation(jax.random.fold_in(own, 3), amount)
    donor, taker = mixed[0:amount // 2 * 2:2], mixed[1:amount // 2 * 2:2]
    room = jnp.minimum(sizes[donor] - 1, bound - sizes[taker]) // 2
    room = jnp.where((donor == order[0]) | (taker == order[0]) | (sizes[taker] == 0), 0, jnp.maximum(room, 0))
    passed = jax.random.randint(jax.random.fold_in(own, 4), (amount // 2,), 0, 1 << 20) % (room + 1)
    sizes = sizes.at[donor].add(-passed).at[taker].add(passed)
    labels = jnp.searchsorted(jnp.cumsum(sizes), jnp.arange(rows * top), side="right").astype(jnp.int32)
    listing = labels.reshape(top, rows).T
    listing = listing[jax.random.permutation(jax.random.fold_in(own, 1), rows)]
    offset_by = jax.random.randint(jax.random.fold_in(own, 2), (rows, 1), 0, top)
    return jnp.take_along_axis(listing, (jnp.arange(top)[None, :] + offset_by) % top, axis=1)


def shares(number_of, total, most, slope, full):
    weights = [(1 << 20) // math.isqrt(rank ** slope) + 1 for rank in range(1, number_of + 1)]
    largest = most if full else min(most, max(-(-total // number_of), total * weights[0] // sum(weights)))
    least = 1 if total - largest >= number_of - 1 else 0
    given, rest = [largest] + [least] * (number_of - 1), total - largest - least * (number_of - 1)
    while rest > 0:
        movable = [i for i in range(1, number_of) if given[i] < largest] or [i for i in range(1, number_of) if given[i] < most]
        pool, remaining = sum([weights[i] for i in movable]), rest
        for i in movable:
            addition = min(most - given[i], max(1, remaining * weights[i] // pool), rest)
            given[i] = given[i] + addition
            rest = rest - addition
    return np.array(given)


def gaussian(own_key, shape, deviation, reach, cuts=(), kind=jnp.bfloat16):
    entries = deviation * jax.random.normal(own_key, shape, jnp.float32)
    if cuts:
        entries = entries * block_levels(own_key, shape, cuts, -0.22, 0.18)
    return jnp.clip(entries, -reach, reach).astype(kind)


def setup_inputs(seed: int = 0) -> dict:
    splits = jax.random.split(jax.random.key(seed), 15)
    qkv = draw_qkv(jax.random.fold_in(splits[14], 71), 0)
    kv_cache = gaussian(splits[1], (N_DP * SLOTS, BLK, HEADS * 2 * HEAD_DIM), 1.0, 6.0, ((0, 64), (2, 8)))
    residual = gaussian(splits[2], (TOKENS, D), 1.0, 6.0, ((0, 64),))
    out_weight = gaussian(splits[3], (HEADS * HEAD_DIM, D), (HEADS * HEAD_DIM) ** -0.5, 0.1875, ((0, 8),))
    moe_gain = jnp.clip(1.0 + 0.18 * jax.random.normal(splits[4], (D,), jnp.float32), 0.1, 1.9)
    w_gate = gaussian(splits[5], (EXPERTS, D, FFE), D ** -0.5, 0.125, ((0, 64), (2, 8)))
    w_up = gaussian(splits[6], (EXPERTS, D, FFE), D ** -0.5, 0.125, ((0, 64), (2, 8)))
    w_down = gaussian(splits[7], (EXPERTS, FFE, D), FFE ** -0.5, 0.15625, ((0, 64), (1, 8)))
    seg_ids = jax.vmap(lambda own: jnp.searchsorted(jnp.cumsum(uneven(own, SEGS, MB, SEG_MOST, 2)), jnp.arange(MB), side="right"))(jax.random.split(splits[8], N_DP * MICRO)).reshape((N_DP, MICRO, MB)).astype(jnp.int32)
    prefix_blocks = jax.vmap(lambda own: uneven(own, SEGS, PREF, PMOST, 2))(jax.random.split(splits[9], N_DP * MICRO)).reshape((N_DP, MICRO, SEGS)).astype(jnp.int32)
    owners_keys = jax.random.split(jax.random.fold_in(splits[10], 1), N_DP * MICRO * PREF // PREF)
    owners_turns = jax.random.permutation(jax.random.fold_in(splits[10], 3), N_DP * MICRO * PREF // PREF)
    owners = jax.vmap(lambda own, number: assign_block(jax.random.fold_in(splits[10], 2), own, number, PREF, N_DP, 1, OWN_CAP, 1))(owners_keys, owners_turns).reshape((N_DP, MICRO, PREF, 1))
    slot_ids = set_ends(jax.random.randint(splits[11], (N_DP, MICRO, PREF), 0, SLOTS), jax.random.fold_in(splits[11], 1), 0, SLOTS - 1).astype(jnp.int32)
    expert_ids_keys = jax.random.split(jax.random.fold_in(splits[12], 1), TOKENS // QROWS)
    expert_ids_turns = jax.random.permutation(jax.random.fold_in(splits[12], 3), TOKENS // QROWS)
    expert_ids = jax.vmap(lambda own, number: assign_block(jax.random.fold_in(splits[12], 2), own, number, QROWS, EXPERTS, TOPK, CAPQ, 0))(expert_ids_keys, expert_ids_turns).reshape((TOKENS, TOPK))
    gate_weights = jnp.clip(jnp.exp(math.log(0.5) - 2.3025851 * jax.random.uniform(splits[13], (TOKENS, TOPK), jnp.float32) ** block_levels(splits[13], (TOKENS, TOPK), ((0, 64),), -0.2, 0.2)), 0.05, 0.5)
    return {"qkv": qkv, "kv_cache": kv_cache, "residual": residual, "out_weight": out_weight, "moe_gain": moe_gain, "w_gate": w_gate, "w_up": w_up, "w_down": w_down, "seg_ids": seg_ids, "prefix_blocks": prefix_blocks, "owners": owners, "slot_ids": slot_ids, "expert_ids": expert_ids, "gate_weights": gate_weights}


def normalize(hidden, gain):
    square = lax.optimization_barrier(jnp.mean(hidden * hidden, axis=-1, keepdims=True))
    return (hidden * lax.rsqrt(square + 1e-06) * gain).astype(jnp.bfloat16)

def attend_block(tokens, segments, counts, owner_row, slot_row, cache_view):
    mb_rows = tokens.shape[0]
    blocks = cache_view[owner_row, slot_row]
    prefix = blocks.reshape(PREF * BLK, HEADS, 2, HEAD_DIM)
    key_rows = jnp.concatenate([prefix[:, :, 0], tokens[:, :, 1]], axis=0).astype(jnp.float32)
    value_rows = jnp.concatenate([prefix[:, :, 1], tokens[:, :, 2]], axis=0).astype(jnp.float32)
    query_rows = tokens[:, :, 0].astype(jnp.float32)
    block_ends = jnp.cumsum(counts)
    block_index = jnp.arange(PREF, dtype=jnp.int32)
    block_seg = lax.optimization_barrier(jnp.sum((block_ends[None, :] <= block_index[:, None]).astype(jnp.int32), axis=1))
    prefix_seg = jnp.repeat(block_seg, BLK)
    position = jnp.arange(mb_rows, dtype=jnp.int32)
    same_prefix = prefix_seg[None, :] == segments[:, None]
    same_new = (segments[None, :] == segments[:, None]) & (position[None, :] <= position[:, None])
    visible = jnp.concatenate([same_prefix, same_new], axis=1)
    scores = jnp.einsum('qhd,khd->hqk', query_rows, key_rows) * (1.0 / math.sqrt(HEAD_DIM))
    scores = jnp.where(visible[None], scores, -jnp.inf)
    row_max = lax.optimization_barrier(jnp.max(scores, axis=2, keepdims=True))
    weights = jnp.exp(scores - row_max)
    probs = (weights / lax.optimization_barrier(jnp.sum(weights, axis=2, keepdims=True))).astype(jnp.bfloat16)
    combined = jnp.einsum('hqk,khd->qhd', probs.astype(jnp.float32), value_rows)
    return combined.astype(jnp.bfloat16).reshape(mb_rows, HEADS * HEAD_DIM)

def reference(qkv, kv_cache, residual, out_weight, moe_gain, w_gate, w_up, w_down, seg_ids, prefix_blocks, owners, slot_ids, expert_ids, gate_weights):
    qkv_view = qkv.reshape(N_DP, MICRO, MB, HEADS, 3, HEAD_DIM)
    cache_view = kv_cache.reshape(N_DP, SLOTS, BLK, HEADS, 2, HEAD_DIM)
    attend_one = partial(attend_block, cache_view=cache_view)
    attended = jax.vmap(jax.vmap(attend_one))(qkv_view, seg_ids, prefix_blocks, owners[..., 0], slot_ids)
    attended = attended.reshape(TOKENS, HEADS * HEAD_DIM)
    attn_proj = jnp.dot(attended, out_weight, preferred_element_type=jnp.float32)
    mixed_in = residual.astype(jnp.float32) + attn_proj
    normed = normalize(mixed_in, moe_gain.astype(jnp.float32))
    block_count = TOKENS // QROWS
    block_ids = expert_ids.reshape(block_count, QROWS * TOPK)
    one_hot = (block_ids[:, :, None] == jnp.arange(EXPERTS, dtype=jnp.int32)[None, None, :]).astype(jnp.int32)
    block_rank = lax.optimization_barrier(jnp.sum((jnp.cumsum(one_hot, axis=1) - one_hot) * one_hot, axis=2))
    block_number = jnp.arange(block_count, dtype=jnp.int32)
    quarter_of = block_number % SPLIT
    micro_group = block_number // SPLIT
    capacity = SPLIT * CAPQ
    buffer_rows = N_DP * MICRO * capacity
    slot_of = quarter_of[:, None] * CAPQ + block_rank
    target = (block_ids * (N_DP * MICRO) + micro_group[:, None]) * capacity + slot_of
    token_index = block_number[:, None] * QROWS + jnp.arange(QROWS * TOPK, dtype=jnp.int32)[None, :] // TOPK
    row_table = jnp.full((EXPERTS * buffer_rows,), TOKENS, jnp.int32).at[target.reshape(-1)].set(token_index.reshape(-1))
    gate_table = jnp.zeros((EXPERTS * buffer_rows,), jnp.float32).at[target.reshape(-1)].set(gate_weights.reshape(-1))
    padded = jnp.concatenate([normed, jnp.zeros((1, D), jnp.bfloat16)], axis=0)
    group_width = FFE // SPLIT

    def one_expert(total, inputs):
        gate_w, up_w, down_w, rows_index, row_gates = inputs
        gathered = padded[rows_index]
        gate_rows = jnp.dot(gathered, gate_w, preferred_element_type=jnp.float32)
        up_rows = jnp.dot(gathered, up_w, preferred_element_type=jnp.float32)
        hidden = (jax.nn.silu(gate_rows) * up_rows).astype(jnp.bfloat16)
        output = jnp.zeros((rows_index.shape[0], D), jnp.float32)
        for piece_index in range(SPLIT):
            lower = piece_index * group_width
            piece_out = jnp.dot(hidden[:, lower:lower + group_width], down_w[lower:lower + group_width], preferred_element_type=jnp.float32)
            rounded = lax.optimization_barrier(piece_out.astype(jnp.bfloat16))
            output = output + rounded.astype(jnp.float32)
        total = total.at[rows_index].add(output * row_gates[:, None])
        return (total, None)
    moe_total, unused = lax.scan(one_expert, jnp.zeros((TOKENS + 1, D), jnp.float32), (w_gate, w_up, w_down, row_table.reshape(EXPERTS, buffer_rows), gate_table.reshape(EXPERTS, buffer_rows)))
    return (mixed_in + moe_total[:TOKENS]).astype(jnp.bfloat16)
```

```python
import math

import jax
import jax.numpy as jnp
from jax import lax
from jax.experimental import pallas as pl
from jax.experimental.pallas import tpu as pltpu
from jax.sharding import PartitionSpec as P

HEAD_DIM = 128
TOPK = 4
PREF = 64
BLK = 8
OWN_CAP = 3
CAPQ = 2
SPLIT = ("section", "mp")


def nt_dot(a, b):
    return lax.dot_general(a, b, (((1,), (1,)), ((), ())), preferred_element_type=jnp.float32)


def attend_kernel(qkv_ref, prefix_ref, key_seg_ref, seg_row_ref, seg_col_ref, weight_ref, out_ref):
    rows = qkv_ref.shape[0]
    query = qkv_ref[:, :HEAD_DIM]
    scale = 1.0 / math.sqrt(HEAD_DIM)
    old = nt_dot(query, prefix_ref[:, :HEAD_DIM]) * scale
    new = nt_dot(query, qkv_ref[:, HEAD_DIM : 2 * HEAD_DIM]) * scale
    seg = seg_col_ref[...]
    earlier = lax.broadcasted_iota(jnp.int32, (rows, rows), 1) <= lax.broadcasted_iota(
        jnp.int32, (rows, rows), 0
    )
    old = jnp.where(key_seg_ref[...] == seg, old, -jnp.inf)
    new = jnp.where((seg_row_ref[...] == seg) & earlier, new, -jnp.inf)
    top = jnp.maximum(
        jnp.max(old, axis=1, keepdims=True), jnp.max(new, axis=1, keepdims=True)
    )
    old = jnp.exp(old - top)
    new = jnp.exp(new - top)
    total = jnp.sum(old, axis=1, keepdims=True) + jnp.sum(new, axis=1, keepdims=True)
    old = (old / total).astype(jnp.bfloat16)
    new = (new / total).astype(jnp.bfloat16)
    attended = jnp.dot(
        old, prefix_ref[:, HEAD_DIM:], preferred_element_type=jnp.float32
    ) + jnp.dot(new, qkv_ref[:, 2 * HEAD_DIM :], preferred_element_type=jnp.float32)
    out_ref[...] = jnp.dot(
        attended.astype(jnp.bfloat16), weight_ref[...], preferred_element_type=jnp.float32
    ).astype(out_ref.dtype)


def norm_kernel(parts_ref, residual_ref, gain_ref, pick_ref, mixed_ref, out_ref):
    mixed = residual_ref[...].astype(jnp.float32)
    projected = parts_ref[0].astype(jnp.float32)
    for i in range(1, parts_ref.shape[0]):
        projected = projected + parts_ref[i].astype(jnp.float32)
    mixed = mixed + projected
    mixed_ref[...] = mixed
    square = jnp.mean(mixed * mixed, axis=1, keepdims=True)
    normed = (mixed * lax.rsqrt(square + 1e-06) * gain_ref[...]).astype(jnp.bfloat16)
    out_ref[...] = jnp.dot(pick_ref[...], normed, preferred_element_type=jnp.float32).astype(
        jnp.bfloat16
    )


def combine_kernel(rows_ref, gate_ref, mixed_ref, out_ref):
    gate = gate_ref[...]
    high = gate.astype(jnp.bfloat16)
    low = (gate - high.astype(jnp.float32)).astype(jnp.bfloat16)
    rows = rows_ref[...]
    total = jnp.dot(high, rows, preferred_element_type=jnp.float32)
    total = total + jnp.dot(low, rows, preferred_element_type=jnp.float32)
    total = (total + mixed_ref[...]).astype(jnp.bfloat16)
    cols = out_ref.shape[2]
    for i in range(out_ref.shape[0]):
        out_ref[i] = total[:, i * cols : (i + 1) * cols]


def local(
    qkv,
    kv_cache,
    residual,
    out_weight,
    moe_gain,
    w_gate,
    w_up,
    w_down,
    seg_ids,
    prefix_blocks,
    owners,
    slot_ids,
    expert_ids,
    gate_weights,
):
    groups = lax.axis_size("dp")
    shards = lax.axis_size("section") * lax.axis_size("mp")
    group = lax.axis_index("dp")
    shard = lax.axis_index("section") * lax.axis_size("mp") + lax.axis_index("mp")
    rows = seg_ids.shape[2]
    block = rows // shards
    width = residual.shape[1]
    cols = width // shards
    slots = groups * CAPQ

    table = owners[:, 0, :, 0]
    owned = table == group
    order = jnp.cumsum(owned.astype(jnp.int32), axis=1) - 1
    wanted = owned[:, None, :] & (
        order[:, None, :] == jnp.arange(OWN_CAP, dtype=jnp.int32)[None, :, None]
    )
    pick = jnp.sum(jnp.where(wanted, slot_ids[:, 0, :][:, None, :], 0), axis=2)
    chosen = kv_cache.at[pick.reshape(-1)].get(mode="promise_in_bounds")
    chosen = chosen.reshape(groups, OWN_CAP, BLK, kv_cache.shape[2])
    arrived = lax.all_to_all(chosen, "dp", split_axis=0, concat_axis=0, tiled=True)

    full_gate = lax.all_gather(w_gate[0].T, SPLIT, axis=0, tiled=True)
    full_up = lax.all_gather(w_up[0].T, SPLIT, axis=0, tiled=True)
    full_down = lax.all_gather(w_down[0], SPLIT, axis=0, tiled=True)

    mine = lax.dynamic_index_in_dim(table, group, 0, keepdims=False)
    index = jnp.arange(PREF, dtype=jnp.int32)
    before = (mine[None, :] == mine[:, None]) & (index[None, :] < index[:, None])
    place = mine * OWN_CAP + jnp.sum(before.astype(jnp.int32), axis=1)
    ends = jnp.cumsum(prefix_blocks[0, 0])
    block_seg = jnp.sum((ends[None, :] <= index[:, None]).astype(jnp.int32), axis=1)
    key_slot = jnp.arange(groups * OWN_CAP * BLK, dtype=jnp.int32) // BLK
    key_seg = (
        jnp.sum(jnp.where(place[:, None] == key_slot[None, :], block_seg[:, None] + 1, 0), axis=0)
        - 1
    )[None, :]
    segments = seg_ids[0, 0]

    first = shard * block
    ids = lax.dynamic_slice_in_dim(expert_ids, first, block, 0)
    gates = lax.dynamic_slice_in_dim(gate_weights, first, block, 0)
    flat = ids.reshape(-1)
    pair = jnp.arange(block * TOPK, dtype=jnp.int32)
    same = (flat[None, :] == flat[:, None]) & (pair[None, :] < pair[:, None])
    slot = (flat * CAPQ + jnp.sum(same.astype(jnp.int32), axis=1)).reshape(block, TOPK)
    slot_index = jnp.arange(slots, dtype=jnp.int32)
    hit = slot[:, :, None] == slot_index[None, None, :]
    gate_matrix = jnp.sum(jnp.where(hit, gates[:, :, None], 0.0), axis=1)
    pick_matrix = jnp.any(slot.T[None, :, :] == slot_index[:, None, None], axis=1).astype(
        jnp.bfloat16
    )
    my_residual = lax.dynamic_slice_in_dim(residual, first, block, 0)

    projected = pl.pallas_call(
        attend_kernel,
        out_shape=jax.ShapeDtypeStruct((rows, width), jnp.bfloat16),
        name="attend",
    )(
        qkv,
        arrived.reshape(-1, kv_cache.shape[2]),
        key_seg,
        segments[None, :],
        segments[:, None],
        out_weight,
    )
    parts = lax.all_to_all(
        projected.reshape(shards, block, width), SPLIT, split_axis=0, concat_axis=0, tiled=True
    )
    mixed, outgoing = pl.pallas_call(
        norm_kernel,
        out_shape=(
            jax.ShapeDtypeStruct((block, width), jnp.float32),
            jax.ShapeDtypeStruct((slots, width), jnp.bfloat16),
        ),
        name="norm",
    )(parts, my_residual, moe_gain[None, :], pick_matrix)
    incoming = lax.all_to_all(
        outgoing.reshape(groups, CAPQ, width), "dp", split_axis=0, concat_axis=0, tiled=True
    ).reshape(slots, width)

    hidden = (jax.nn.silu(nt_dot(incoming, full_gate)) * nt_dot(incoming, full_up)).astype(
        jnp.bfloat16
    )
    produced = jnp.dot(hidden, full_down, preferred_element_type=jnp.float32).astype(jnp.bfloat16)
    returned = lax.all_to_all(
        produced.reshape(groups, CAPQ, width), "dp", split_axis=0, concat_axis=0, tiled=True
    ).reshape(slots, width)
    finished = pl.pallas_call(
        combine_kernel,
        out_shape=jax.ShapeDtypeStruct((shards, block, cols), jnp.bfloat16),
        name="combine",
    )(returned, gate_matrix, mixed)
    result = lax.all_to_all(finished, SPLIT, split_axis=0, concat_axis=0, tiled=True)
    return result.reshape(rows, cols)


def solution(mesh):
    return jax.shard_map(
        local,
        mesh=mesh,
        in_specs=(
            P("dp", ("section", "mp")),
            P("dp", None, ("section", "mp")),
            P("dp", None),
            P(("section", "mp"), None),
            P(),
            P("dp", None, ("section", "mp")),
            P("dp", None, ("section", "mp")),
            P("dp", ("section", "mp"), None),
            P("dp", None, None),
            P("dp", None, None),
            P(),
            P(),
            P("dp", None),
            P("dp", None),
        ),
        out_specs=P("dp", ("section", "mp")),
        check_vma=False,
    )
```

```python
import math

import jax
import jax.numpy as jnp
from jax import lax
from jax.experimental import pallas as pl
from jax.experimental.pallas import tpu as pltpu
from jax.sharding import PartitionSpec as P

HEAD_DIM = 128
LANES = 128
TOPK = 4
PREF = 64
BLK = 8
OWN_CAP = 3
CAPQ = 2
PIECES = 4
CHUNKS = (2, 2, 2, 1, 1)
SPLIT = ("section", "mp")


def nt_dot(a, b):
    return lax.dot_general(a, b, (((1,), (1,)), ((), ())), preferred_element_type=jnp.float32)


def attend_kernel(qkv_ref, prefix_ref, key_seg_ref, seg_row_ref, seg_col_ref, weight_ref, out_ref):
    rows = qkv_ref.shape[0]
    query = qkv_ref[:, :HEAD_DIM]
    scale = 1.0 / math.sqrt(HEAD_DIM)
    old = nt_dot(query, prefix_ref[:, :HEAD_DIM]) * scale
    new = nt_dot(query, qkv_ref[:, HEAD_DIM : 2 * HEAD_DIM]) * scale
    seg = seg_col_ref[...]
    earlier = lax.broadcasted_iota(jnp.int32, (rows, rows), 1) <= lax.broadcasted_iota(
        jnp.int32, (rows, rows), 0
    )
    old = jnp.where(key_seg_ref[...] == seg, old, -jnp.inf)
    new = jnp.where((seg_row_ref[...] == seg) & earlier, new, -jnp.inf)
    top = jnp.maximum(
        jnp.max(old, axis=1, keepdims=True), jnp.max(new, axis=1, keepdims=True)
    )
    old = jnp.exp(old - top)
    new = jnp.exp(new - top)
    total = jnp.sum(old, axis=1, keepdims=True) + jnp.sum(new, axis=1, keepdims=True)
    old = (old / total).astype(jnp.bfloat16)
    new = (new / total).astype(jnp.bfloat16)
    attended = jnp.dot(
        old, prefix_ref[:, HEAD_DIM:], preferred_element_type=jnp.float32
    ) + jnp.dot(new, qkv_ref[:, 2 * HEAD_DIM :], preferred_element_type=jnp.float32)
    out_ref[...] = jnp.dot(
        attended.astype(jnp.bfloat16), weight_ref[...], preferred_element_type=jnp.float32
    ).astype(out_ref.dtype)


def in_vmem(x):
    return pltpu.with_memory_space_constraint(x, pltpu.VMEM)


def in_hbm(x):
    return pltpu.with_memory_space_constraint(x, pltpu.HBM)


def select_kernel(
    owners_ref,
    slots_ref,
    cache_ref,
    gate_hbm,
    up_hbm,
    down_hbm,
    out_ref,
    pack_hbm,
    cache_wide,
    out_wide,
    pack_buf,
    sems,
):
    unit = gate_hbm.shape[0]
    parts = [pl.ds(i * unit, unit) for i in range(3)]
    loads = [
        pltpu.make_async_copy(source, pack_buf.at[part], sems.at[0, i])
        for i, (source, part) in enumerate(zip((gate_hbm, up_hbm, down_hbm), parts))
    ]
    stores = [
        pltpu.make_async_copy(pack_buf.at[part], pack_hbm.at[part], sems.at[1, i])
        for i, part in enumerate(parts)
    ]
    for load in loads:
        load.start()
    halves = cache_wide.shape[0]
    for h in range(halves):
        cache_wide[h] = cache_ref[:, h * LANES : (h + 1) * LANES].astype(jnp.float32)
    owned = owners_ref[:, 0, :] == lax.axis_index("dp")
    named = slots_ref[:, 0, :]
    groups, entries = owned.shape
    earlier = lax.broadcasted_iota(jnp.int32, (entries, entries), 0) < lax.broadcasted_iota(
        jnp.int32, (entries, entries), 1
    )
    rank = jnp.dot(
        jnp.where(owned, 1.0, 0.0).astype(jnp.bfloat16),
        jnp.where(earlier, 1.0, 0.0).astype(jnp.bfloat16),
        preferred_element_type=jnp.float32,
    )
    held = cache_ref.shape[0] // BLK
    index = lax.broadcasted_iota(jnp.int32, (groups, held), 1)
    picks = []
    for r in range(OWN_CAP):
        slot = jnp.sum(jnp.where(owned & (rank == r), named, 0), axis=1, keepdims=True)
        picks.append(jnp.where(slot == index, 1.0, 0.0).astype(jnp.bfloat16))
    picks = jnp.concatenate(picks, axis=0)
    for load, store in zip(loads, stores):
        load.wait()
        store.start()
    for b in range(BLK):
        part = jnp.concatenate(
            [cache_wide[h, pl.ds(b, held, stride=BLK), :] for h in range(halves)], axis=1
        )
        chosen = jnp.dot(picks, part.astype(jnp.bfloat16), preferred_element_type=jnp.float32)
        for r in range(OWN_CAP):
            for h in range(halves):
                out_wide[h, pl.ds(r * BLK + b, groups, stride=OWN_CAP * BLK), :] = chosen[
                    r * groups : (r + 1) * groups, h * LANES : (h + 1) * LANES
                ]
    for h in range(halves):
        out_ref[:, h * LANES : (h + 1) * LANES] = out_wide[h].astype(jnp.bfloat16)
    for store in stores:
        store.wait()


def norm_kernel(parts_ref, residual_ref, gain_ref, pick_ref, mixed_ref, out_ref):
    mixed = residual_ref[...].astype(jnp.float32)
    projected = parts_ref[0].astype(jnp.float32)
    for i in range(1, parts_ref.shape[0]):
        projected = projected + parts_ref[i].astype(jnp.float32)
    mixed = mixed + projected
    mixed_ref[...] = mixed
    square = jnp.mean(mixed * mixed, axis=1, keepdims=True)
    normed = (mixed * lax.rsqrt(square + 1e-06) * gain_ref[...]).astype(jnp.bfloat16)
    out_ref[...] = jnp.dot(
        pick_ref[...], stack_pieces(normed), preferred_element_type=jnp.float32
    ).astype(jnp.bfloat16)


def stack_pieces(x):
    cols = x.shape[1] // PIECES
    return jnp.concatenate([x[:, i * cols : (i + 1) * cols] for i in range(PIECES)], axis=0)


def join_pieces(x):
    rows = x.shape[0] // PIECES
    return jnp.concatenate([x[i * rows : (i + 1) * rows] for i in range(PIECES)], axis=1)


def ffn_kernel(x_ref, weight_hbm, out_ref, weight_ref, sems):
    shards, _, unit, width = weight_ref.shape
    ends = [sum(CHUNKS[: i + 1]) for i in range(len(CHUNKS))]
    spans = [(end - size, size) for end, size in zip(ends, CHUNKS)]
    assert ends[-1] == shards
    copies = [
        pltpu.make_async_copy(
            weight_hbm.at[pl.ds(first, size)], weight_ref.at[pl.ds(first, size)], sems.at[i]
        )
        for i, (first, size) in enumerate(spans)
    ]
    ahead = 3
    for copy in copies[:ahead]:
        copy.start()
    total = x_ref.shape[0]
    rows = total // PIECES
    near = lax.broadcasted_iota(jnp.int32, (total, total), 0)
    far = lax.broadcasted_iota(jnp.int32, (total, total), 1)
    to_rows = jnp.where(far == (near % rows) * PIECES + near // rows, 1.0, 0.0).astype(jnp.bfloat16)
    to_pieces = jnp.where(near == (far % rows) * PIECES + far // rows, 1.0, 0.0).astype(
        jnp.bfloat16
    )
    x = join_pieces(
        jnp.dot(to_rows, x_ref[...], preferred_element_type=jnp.float32).astype(jnp.bfloat16)
    )
    result = jnp.zeros((rows, width), jnp.float32)
    for i, (first, size) in enumerate(spans):
        copies[i].wait()
        if i + ahead < len(copies):
            copies[i + ahead].start()
        gate, up, down = (
            weight_ref[first : first + size, j].reshape(size * unit, width) for j in range(3)
        )
        gate = nt_dot(x, gate)
        hidden = (gate / (1.0 + jnp.exp(-gate)) * nt_dot(x, up)).astype(jnp.bfloat16)
        result = result + jnp.dot(hidden, down, preferred_element_type=jnp.float32)
    out_ref[...] = jnp.dot(
        to_pieces, stack_pieces(result.astype(jnp.bfloat16)), preferred_element_type=jnp.float32
    ).astype(jnp.bfloat16)


def combine_kernel(rows_ref, gate_ref, mixed_ref, out_ref):
    gate = gate_ref[...]
    high = gate.astype(jnp.bfloat16)
    low = (gate - high.astype(jnp.float32)).astype(jnp.bfloat16)
    rows = rows_ref[...]
    total = jnp.dot(high, rows, preferred_element_type=jnp.float32)
    total = total + jnp.dot(low, rows, preferred_element_type=jnp.float32)
    total = (join_pieces(total) + mixed_ref[...]).astype(jnp.bfloat16)
    cols = out_ref.shape[2]
    for i in range(out_ref.shape[0]):
        out_ref[i] = total[:, i * cols : (i + 1) * cols]


def local(
    qkv,
    kv_cache,
    residual,
    out_weight,
    moe_gain,
    w_gate,
    w_up,
    w_down,
    seg_ids,
    prefix_blocks,
    owners,
    slot_ids,
    expert_ids,
    gate_weights,
):
    groups = lax.axis_size("dp")
    shards = lax.axis_size("section") * lax.axis_size("mp")
    group = lax.axis_index("dp")
    shard = lax.axis_index("section") * lax.axis_size("mp") + lax.axis_index("mp")
    rows = seg_ids.shape[2]
    block = rows // shards
    width = residual.shape[1]
    cols = width // shards
    slots = groups * CAPQ

    vmem = pl.BlockSpec(memory_space=pltpu.VMEM)
    hbm = pl.BlockSpec(memory_space=pltpu.HBM)
    table = owners[:, 0, :, 0]
    unit = w_down.shape[1]
    cache_cols = kv_cache.shape[2]
    cache_rows = kv_cache.shape[0] * BLK
    sent_rows = groups * OWN_CAP * BLK
    chosen, packed = pl.pallas_call(
        select_kernel,
        in_specs=[vmem, vmem, vmem, hbm, hbm, hbm],
        out_specs=(vmem, hbm),
        out_shape=(
            pltpu.VMEM((sent_rows, cache_cols), jnp.bfloat16),
            pltpu.HBM((3 * unit, width), jnp.bfloat16),
        ),
        scratch_shapes=[
            pltpu.VMEM((cache_cols // LANES, cache_rows, LANES), jnp.float32),
            pltpu.VMEM((cache_cols // LANES, sent_rows, LANES), jnp.float32),
            pltpu.VMEM((3 * unit, width), jnp.bfloat16),
            pltpu.SemaphoreType.DMA((2, 3)),
        ],
        compiler_params=pltpu.CompilerParams(vmem_limit_bytes=12 << 20),
        name="select",
    )(
        in_hbm(owners[:, :, :, 0]),
        in_hbm(slot_ids),
        in_hbm(kv_cache.reshape(cache_rows, cache_cols)),
        in_hbm(w_gate[0].T),
        in_hbm(w_up[0].T),
        in_hbm(w_down[0]),
    )
    arrived = lax.all_to_all(
        chosen.reshape(groups, OWN_CAP, BLK, cache_cols),
        "dp",
        split_axis=0,
        concat_axis=0,
        tiled=True,
    )
    full = lax.all_gather(packed, SPLIT, axis=0, tiled=True)

    mine = lax.dynamic_index_in_dim(table, group, 0, keepdims=False)
    index = jnp.arange(PREF, dtype=jnp.int32)
    before = (mine[None, :] == mine[:, None]) & (index[None, :] < index[:, None])
    place = mine * OWN_CAP + jnp.sum(before.astype(jnp.int32), axis=1)
    ends = jnp.cumsum(prefix_blocks[0, 0])
    block_seg = jnp.sum((ends[None, :] <= index[:, None]).astype(jnp.int32), axis=1)
    key_slot = jnp.arange(groups * OWN_CAP * BLK, dtype=jnp.int32) // BLK
    key_seg = (
        jnp.sum(jnp.where(place[:, None] == key_slot[None, :], block_seg[:, None] + 1, 0), axis=0)
        - 1
    )[None, :]
    segments = seg_ids[0, 0]

    first = shard * block
    ids = lax.dynamic_slice_in_dim(expert_ids, first, block, 0)
    gates = lax.dynamic_slice_in_dim(gate_weights, first, block, 0)
    flat = ids.reshape(-1)
    pair = jnp.arange(block * TOPK, dtype=jnp.int32)
    same = (flat[None, :] == flat[:, None]) & (pair[None, :] < pair[:, None])
    slot = (flat * CAPQ + jnp.sum(same.astype(jnp.int32), axis=1)).reshape(block, TOPK)
    slot_index = jnp.arange(slots, dtype=jnp.int32)
    line = jnp.arange(slots * PIECES, dtype=jnp.int32)
    piece = jnp.arange(PIECES, dtype=jnp.int32)
    hit = slot[:, :, None] == line[None, None, :] // PIECES
    mine_of_piece = (line[None, :] % PIECES == piece[:, None])[:, None, :]
    gate_matrix = jnp.where(
        mine_of_piece, jnp.sum(jnp.where(hit, gates[:, :, None], 0.0), axis=1)[None], 0.0
    ).reshape(PIECES * block, -1)
    pick_matrix = (
        (mine_of_piece & jnp.any(hit, axis=1)[None]).reshape(PIECES * block, -1).T
    ).astype(jnp.bfloat16)
    my_residual = lax.dynamic_slice_in_dim(residual, first, block, 0)

    lines = slots * PIECES
    piece_cols = width // PIECES
    projected = pl.pallas_call(
        attend_kernel,
        in_specs=[vmem] * 6,
        out_specs=vmem,
        out_shape=pltpu.VMEM((rows, width), jnp.bfloat16),
        name="attend",
    )(
        in_hbm(qkv),
        in_vmem(arrived.reshape(-1, kv_cache.shape[2])),
        in_vmem(key_seg),
        in_hbm(segments[None, :]),
        in_vmem(segments[:, None]),
        in_hbm(out_weight),
    )
    parts = lax.all_to_all(
        projected.reshape(shards, block, width), SPLIT, split_axis=0, concat_axis=0, tiled=True
    )
    mixed, outgoing = pl.pallas_call(
        norm_kernel,
        in_specs=[vmem] * 4,
        out_specs=(vmem, vmem),
        out_shape=(
            pltpu.VMEM((block, width), jnp.float32),
            pltpu.VMEM((lines, piece_cols), jnp.bfloat16),
        ),
        name="norm",
    )(in_vmem(parts), in_vmem(my_residual), in_hbm(moe_gain[None, :]), in_vmem(pick_matrix))
    incoming = lax.all_to_all(
        outgoing.reshape(groups, CAPQ * PIECES, piece_cols),
        "dp",
        split_axis=0,
        concat_axis=0,
        tiled=True,
    ).reshape(lines, piece_cols)

    produced = pl.pallas_call(
        ffn_kernel,
        in_specs=[vmem, hbm],
        out_specs=vmem,
        out_shape=pltpu.VMEM((lines, piece_cols), jnp.bfloat16),
        scratch_shapes=[
            pltpu.VMEM((shards, 3, unit, width), jnp.bfloat16),
            pltpu.SemaphoreType.DMA((len(CHUNKS),)),
        ],
        compiler_params=pltpu.CompilerParams(vmem_limit_bytes=40 << 20),
        name="ffn",
    )(in_vmem(incoming), in_hbm(full.reshape(shards, 3, unit, width)))
    returned = lax.all_to_all(
        produced.reshape(groups, CAPQ * PIECES, piece_cols),
        "dp",
        split_axis=0,
        concat_axis=0,
        tiled=True,
    ).reshape(lines, piece_cols)
    finished = pl.pallas_call(
        combine_kernel,
        in_specs=[vmem] * 3,
        out_specs=vmem,
        out_shape=pltpu.VMEM((shards, block, cols), jnp.bfloat16),
        name="combine",
    )(in_vmem(returned), in_vmem(gate_matrix), in_vmem(mixed))
    result = lax.all_to_all(finished, SPLIT, split_axis=0, concat_axis=0, tiled=True)
    return result.reshape(rows, cols)


def solution(mesh):
    return jax.shard_map(
        local,
        mesh=mesh,
        in_specs=(
            P("dp", ("section", "mp")),
            P("dp", None, ("section", "mp")),
            P("dp", None),
            P(("section", "mp"), None),
            P(),
            P("dp", None, ("section", "mp")),
            P("dp", None, ("section", "mp")),
            P("dp", ("section", "mp"), None),
            P("dp", None, None),
            P("dp", None, None),
            P(),
            P(),
            P("dp", None),
            P("dp", None),
        ),
        out_specs=P("dp", ("section", "mp")),
        check_vma=False,
    )
```

```python
import math

import jax
import jax.numpy as jnp
from jax import lax
from jax.experimental import pallas as pl
from jax.experimental.pallas import tpu as pltpu
from jax.sharding import PartitionSpec as P

HEAD_DIM = 128
LANES = 128
TOPK = 4
PREF = 64
BLK = 8
OWN_CAP = 3
CAPQ = 2
PIECES = 4
CHUNKS = (2, 2, 2, 1, 1)
SPLIT = ("section", "mp")


def nt_dot(a, b):
    return lax.dot_general(a, b, (((1,), (1,)), ((), ())), preferred_element_type=jnp.float32)


def attend_kernel(
    qkv_ref, prefix_ref, key_seg_ref, seg_row_ref, seg_col_ref, weight_ref, keep_ref, send_ref, rows_ref
):
    rows = qkv_ref.shape[0]
    query = qkv_ref[:, :HEAD_DIM]
    scale = 1.0 / math.sqrt(HEAD_DIM)
    old = nt_dot(query, prefix_ref[:, :HEAD_DIM]) * scale
    new = nt_dot(query, qkv_ref[:, HEAD_DIM : 2 * HEAD_DIM]) * scale
    seg = seg_col_ref[...]
    earlier = lax.broadcasted_iota(jnp.int32, (rows, rows), 1) <= lax.broadcasted_iota(
        jnp.int32, (rows, rows), 0
    )
    old = jnp.where(key_seg_ref[...] == seg, old, -jnp.inf)
    new = jnp.where((seg_row_ref[...] == seg) & earlier, new, -jnp.inf)
    top = jnp.maximum(
        jnp.max(old, axis=1, keepdims=True), jnp.max(new, axis=1, keepdims=True)
    )
    old = jnp.exp(old - top)
    new = jnp.exp(new - top)
    total = jnp.sum(old, axis=1, keepdims=True) + jnp.sum(new, axis=1, keepdims=True)
    old = (old / total).astype(jnp.bfloat16)
    new = (new / total).astype(jnp.bfloat16)
    attended = jnp.dot(
        old, prefix_ref[:, HEAD_DIM:], preferred_element_type=jnp.float32
    ) + jnp.dot(new, qkv_ref[:, 2 * HEAD_DIM :], preferred_element_type=jnp.float32)
    rows_ref[...] = attended.astype(jnp.bfloat16)
    half = keep_ref.shape[0]
    core = lax.axis_index("section")
    for ref, side in ((keep_ref, core), (send_ref, 1 - core)):
        part = rows_ref[pl.ds(pl.multiple_of(side * half, half), half), :]
        ref[...] = jnp.dot(
            part, weight_ref[...], preferred_element_type=jnp.float32
        ).astype(ref.dtype)


def add_kernel(a_ref, b_ref, out_ref):
    out_ref[...] = (a_ref[...] + b_ref[...].astype(jnp.float32)).astype(out_ref.dtype)


def in_vmem(x):
    return pltpu.with_memory_space_constraint(x, pltpu.VMEM)


def in_hbm(x):
    return pltpu.with_memory_space_constraint(x, pltpu.HBM)


def fetch_kernel(*refs):
    count = len(refs) // 2
    sems = refs[-1]
    copies = [
        pltpu.make_async_copy(refs[i], refs[count + i], sems.at[i]) for i in range(count)
    ]
    for copy in copies:
        copy.start()
    for copy in copies:
        copy.wait()


def select_kernel(
    owners_hbm,
    slots_hbm,
    cache_hbm,
    gate_hbm,
    up_hbm,
    down_hbm,
    out_hbm,
    pack_hbm,
    owners_ref,
    slots_ref,
    cache_ref,
    cache_wide,
    out_wide,
    out_ref,
    pack_buf,
    table_sems,
    load_sems,
    store_sems,
    out_sems,
):
    unit = gate_hbm.shape[0]
    tables = [
        pltpu.make_async_copy(source, target, table_sems.at[i])
        for i, (source, target) in enumerate(
            ((owners_hbm, owners_ref), (slots_hbm, slots_ref), (cache_hbm, cache_ref))
        )
    ]
    parts = [pl.ds(i * unit, unit) for i in range(3)]
    loads = [
        pltpu.make_async_copy(source, pack_buf.at[part], load_sems.at[i])
        for i, (source, part) in enumerate(zip((gate_hbm, up_hbm, down_hbm), parts))
    ]
    stores = [
        pltpu.make_async_copy(pack_buf.at[part], pack_hbm.at[part], store_sems.at[i])
        for i, part in enumerate(parts)
    ]
    for copy in tables + loads:
        copy.start()
    tables[0].wait()
    owned = owners_ref[:, 0, :] == lax.axis_index("dp")
    groups, entries = owned.shape
    earlier = lax.broadcasted_iota(jnp.int32, (entries, entries), 0) < lax.broadcasted_iota(
        jnp.int32, (entries, entries), 1
    )
    rank = jnp.dot(
        jnp.where(owned, 1.0, 0.0).astype(jnp.bfloat16),
        jnp.where(earlier, 1.0, 0.0).astype(jnp.bfloat16),
        preferred_element_type=jnp.float32,
    )
    tables[1].wait()
    named = slots_ref[:, 0, :]
    held = cache_ref.shape[0] // BLK
    index = lax.broadcasted_iota(jnp.int32, (groups, held), 1)
    picks = []
    for r in range(OWN_CAP):
        slot = jnp.sum(jnp.where(owned & (rank == r), named, 0), axis=1, keepdims=True)
        picks.append(jnp.where(slot == index, 1.0, 0.0).astype(jnp.bfloat16))
    picks = jnp.concatenate(picks, axis=0)
    tables[2].wait()
    halves = cache_wide.shape[0]
    for h in range(halves):
        cache_wide[h] = cache_ref[:, h * LANES : (h + 1) * LANES].astype(jnp.float32)
    for load, store in zip(loads, stores):
        load.wait()
        store.start()
    outs = []
    for h in range(halves):
        for b in range(BLK):
            part = cache_wide[h, pl.ds(b, held, stride=BLK), :].astype(jnp.bfloat16)
            chosen = jnp.dot(picks, part, preferred_element_type=jnp.float32)
            for r in range(OWN_CAP):
                out_wide[h, pl.ds(r * BLK + b, groups, stride=OWN_CAP * BLK), :] = chosen[
                    r * groups : (r + 1) * groups
                ]
        out_ref[h] = out_wide[h].astype(jnp.bfloat16)
        outs.append(
            pltpu.make_async_copy(
                out_ref.at[h], out_hbm.at[:, pl.ds(h * LANES, LANES)], out_sems.at[h]
            )
        )
        outs[-1].start()
    for copy in outs + stores:
        copy.wait()


def norm_kernel(parts_ref, residual_ref, gain_ref, pick_ref, mixed_ref, out_ref):
    mixed = residual_ref[...].astype(jnp.float32)
    projected = parts_ref[0].astype(jnp.float32)
    for i in range(1, parts_ref.shape[0]):
        projected = projected + parts_ref[i].astype(jnp.float32)
    mixed = mixed + projected
    mixed_ref[...] = mixed
    square = jnp.mean(mixed * mixed, axis=1, keepdims=True)
    normed = (mixed * lax.rsqrt(square + 1e-06) * gain_ref[...]).astype(jnp.bfloat16)
    out_ref[...] = jnp.dot(
        pick_ref[...], stack_pieces(normed), preferred_element_type=jnp.float32
    ).astype(jnp.bfloat16)


def stack_pieces(x):
    cols = x.shape[1] // PIECES
    return jnp.concatenate([x[:, i * cols : (i + 1) * cols] for i in range(PIECES)], axis=0)


def join_pieces(x):
    rows = x.shape[0] // PIECES
    return jnp.concatenate([x[i * rows : (i + 1) * rows] for i in range(PIECES)], axis=1)


def ffn_kernel(x_ref, weight_hbm, out_ref, weight_ref, sems):
    shards, _, unit, width = weight_ref.shape
    ends = [sum(CHUNKS[: i + 1]) for i in range(len(CHUNKS))]
    spans = [(end - size, size) for end, size in zip(ends, CHUNKS)]
    assert ends[-1] == shards
    copies = [
        pltpu.make_async_copy(
            weight_hbm.at[pl.ds(first, size)], weight_ref.at[pl.ds(first, size)], sems.at[i]
        )
        for i, (first, size) in enumerate(spans)
    ]
    ahead = 3
    for copy in copies[:ahead]:
        copy.start()
    total = x_ref.shape[0]
    rows = total // PIECES
    near = lax.broadcasted_iota(jnp.int32, (total, total), 0)
    far = lax.broadcasted_iota(jnp.int32, (total, total), 1)
    to_rows = jnp.where(far == (near % rows) * PIECES + near // rows, 1.0, 0.0).astype(jnp.bfloat16)
    to_pieces = jnp.where(near == (far % rows) * PIECES + far // rows, 1.0, 0.0).astype(
        jnp.bfloat16
    )
    x = join_pieces(
        jnp.dot(to_rows, x_ref[...], preferred_element_type=jnp.float32).astype(jnp.bfloat16)
    )
    result = jnp.zeros((rows, width), jnp.float32)
    for i, (first, size) in enumerate(spans):
        copies[i].wait()
        if i + ahead < len(copies):
            copies[i + ahead].start()
        gate, up, down = (
            weight_ref[first : first + size, j].reshape(size * unit, width) for j in range(3)
        )
        gate = nt_dot(x, gate)
        hidden = (gate / (1.0 + jnp.exp(-gate)) * nt_dot(x, up)).astype(jnp.bfloat16)
        result = result + jnp.dot(hidden, down, preferred_element_type=jnp.float32)
    out_ref[...] = jnp.dot(
        to_pieces, stack_pieces(result.astype(jnp.bfloat16)), preferred_element_type=jnp.float32
    ).astype(jnp.bfloat16)


def combine_kernel(rows_ref, gate_ref, mixed_ref, out_ref):
    gate = gate_ref[...]
    high = gate.astype(jnp.bfloat16)
    low = (gate - high.astype(jnp.float32)).astype(jnp.bfloat16)
    rows = rows_ref[...]
    total = jnp.dot(high, rows, preferred_element_type=jnp.float32)
    total = total + jnp.dot(low, rows, preferred_element_type=jnp.float32)
    total = (join_pieces(total) + mixed_ref[...]).astype(jnp.bfloat16)
    cols = out_ref.shape[2]
    for i in range(out_ref.shape[0]):
        out_ref[i] = total[:, i * cols : (i + 1) * cols]


def local(
    qkv,
    kv_cache,
    residual,
    out_weight,
    moe_gain,
    w_gate,
    w_up,
    w_down,
    seg_ids,
    prefix_blocks,
    owners,
    slot_ids,
    expert_ids,
    gate_weights,
):
    groups = lax.axis_size("dp")
    shards = lax.axis_size("section") * lax.axis_size("mp")
    group = lax.axis_index("dp")
    shard = lax.axis_index("section") * lax.axis_size("mp") + lax.axis_index("mp")
    rows = seg_ids.shape[2]
    block = rows // shards
    width = residual.shape[1]
    cols = width // shards
    slots = groups * CAPQ

    vmem = pl.BlockSpec(memory_space=pltpu.VMEM)
    hbm = pl.BlockSpec(memory_space=pltpu.HBM)
    table = owners[:, 0, :, 0]
    unit = w_down.shape[1]
    cache_cols = kv_cache.shape[2]
    cache_rows = kv_cache.shape[0] * BLK
    sent_rows = groups * OWN_CAP * BLK
    chosen, packed = pl.pallas_call(
        select_kernel,
        in_specs=[hbm] * 6,
        out_specs=(hbm, hbm),
        out_shape=(
            pltpu.HBM((sent_rows, cache_cols), jnp.bfloat16),
            pltpu.HBM((3 * unit, width), jnp.bfloat16),
        ),
        scratch_shapes=[
            pltpu.VMEM((groups, 1, PREF), jnp.int32),
            pltpu.VMEM((groups, 1, PREF), jnp.int32),
            pltpu.VMEM((cache_rows, cache_cols), jnp.bfloat16),
            pltpu.VMEM((cache_cols // LANES, cache_rows, LANES), jnp.float32),
            pltpu.VMEM((cache_cols // LANES, sent_rows, LANES), jnp.float32),
            pltpu.VMEM((cache_cols // LANES, sent_rows, LANES), jnp.bfloat16),
            pltpu.VMEM((3 * unit, width), jnp.bfloat16),
            pltpu.SemaphoreType.DMA((3,)),
            pltpu.SemaphoreType.DMA((3,)),
            pltpu.SemaphoreType.DMA((3,)),
            pltpu.SemaphoreType.DMA((cache_cols // LANES,)),
        ],
        compiler_params=pltpu.CompilerParams(vmem_limit_bytes=12 << 20),
        name="select",
    )(
        in_hbm(owners[:, :, :, 0]),
        in_hbm(slot_ids),
        in_hbm(kv_cache.reshape(cache_rows, cache_cols)),
        in_hbm(w_gate[0].T),
        in_hbm(w_up[0].T),
        in_hbm(w_down[0]),
    )
    arrived = lax.all_to_all(
        chosen.reshape(groups, OWN_CAP, BLK, cache_cols),
        "dp",
        split_axis=0,
        concat_axis=0,
        tiled=True,
    )
    full = lax.all_gather(packed, SPLIT, axis=0, tiled=True)

    mine = lax.dynamic_index_in_dim(table, group, 0, keepdims=False)
    index = jnp.arange(PREF, dtype=jnp.int32)
    before = (mine[None, :] == mine[:, None]) & (index[None, :] < index[:, None])
    place = mine * OWN_CAP + jnp.sum(before.astype(jnp.int32), axis=1)
    ends = jnp.cumsum(prefix_blocks[0, 0])
    block_seg = jnp.sum((ends[None, :] <= index[:, None]).astype(jnp.int32), axis=1)
    key_slot = jnp.arange(groups * OWN_CAP * BLK, dtype=jnp.int32) // BLK
    key_seg = (
        jnp.sum(jnp.where(place[:, None] == key_slot[None, :], block_seg[:, None] + 1, 0), axis=0)
        - 1
    )[None, :]
    segments = seg_ids[0, 0]

    first = shard * block
    ids = lax.dynamic_slice_in_dim(expert_ids, first, block, 0)
    gates = lax.dynamic_slice_in_dim(gate_weights, first, block, 0)
    flat = ids.reshape(-1)
    pair = jnp.arange(block * TOPK, dtype=jnp.int32)
    same = (flat[None, :] == flat[:, None]) & (pair[None, :] < pair[:, None])
    slot = (flat * CAPQ + jnp.sum(same.astype(jnp.int32), axis=1)).reshape(block, TOPK)
    slot_index = jnp.arange(slots, dtype=jnp.int32)
    line = jnp.arange(slots * PIECES, dtype=jnp.int32)
    piece = jnp.arange(PIECES, dtype=jnp.int32)
    hit = slot[:, :, None] == line[None, None, :] // PIECES
    mine_of_piece = (line[None, :] % PIECES == piece[:, None])[:, None, :]
    gate_matrix = jnp.where(
        mine_of_piece, jnp.sum(jnp.where(hit, gates[:, :, None], 0.0), axis=1)[None], 0.0
    ).reshape(PIECES * block, -1)
    pick_matrix = (
        (mine_of_piece & jnp.any(hit, axis=1)[None]).reshape(PIECES * block, -1).T
    ).astype(jnp.bfloat16)
    my_residual = lax.dynamic_slice_in_dim(residual, first, block, 0)

    near = (qkv, out_weight, moe_gain[None, :])
    near = pl.pallas_call(
        fetch_kernel,
        in_specs=[hbm] * len(near),
        out_specs=(vmem,) * len(near),
        out_shape=tuple(pltpu.VMEM(x.shape, x.dtype) for x in near),
        scratch_shapes=[pltpu.SemaphoreType.DMA((len(near),))],
        compiler_params=pltpu.CompilerParams(vmem_limit_bytes=1 << 20),
        name="fetch",
    )(*[in_hbm(x) for x in near])
    arrived, near, pick_matrix, gate_matrix, my_residual = lax.optimization_barrier(
        (arrived, near, pick_matrix, gate_matrix, my_residual)
    )
    near_qkv, near_weight, near_gain = near
    lines = slots * PIECES
    piece_cols = width // PIECES
    half = rows // lax.axis_size("section")
    kept, sent = pl.pallas_call(
        attend_kernel,
        in_specs=[vmem] * 6,
        out_specs=(vmem, vmem),
        out_shape=(
            pltpu.VMEM((half, width), jnp.float32),
            pltpu.VMEM((half, width), jnp.bfloat16),
        ),
        scratch_shapes=[pltpu.VMEM((rows, HEAD_DIM), jnp.bfloat16)],
        compiler_params=pltpu.CompilerParams(vmem_limit_bytes=16 << 20),
        name="attend",
    )(
        in_vmem(near_qkv),
        in_vmem(arrived.reshape(-1, kv_cache.shape[2])),
        in_vmem(key_seg),
        in_hbm(segments[None, :]),
        in_vmem(segments[:, None]),
        in_vmem(near_weight),
    )
    received = lax.ppermute(sent, "section", [(0, 1), (1, 0)])
    projected = pl.pallas_call(
        add_kernel,
        in_specs=[vmem, vmem],
        out_specs=vmem,
        out_shape=pltpu.VMEM((half, width), jnp.bfloat16),
        compiler_params=pltpu.CompilerParams(vmem_limit_bytes=4 << 20),
        name="add",
    )(in_vmem(kept), in_vmem(received))
    chips = lax.axis_size("mp")
    parts = lax.all_to_all(
        projected.reshape(chips, block, width), "mp", split_axis=0, concat_axis=0, tiled=True
    )
    mixed, outgoing = pl.pallas_call(
        norm_kernel,
        in_specs=[vmem] * 4,
        out_specs=(vmem, vmem),
        out_shape=(
            pltpu.VMEM((block, width), jnp.float32),
            pltpu.VMEM((lines, piece_cols), jnp.bfloat16),
        ),
        compiler_params=pltpu.CompilerParams(vmem_limit_bytes=8 << 20),
        name="norm",
    )(in_vmem(parts), in_vmem(my_residual), in_vmem(near_gain), in_vmem(pick_matrix))
    incoming = lax.all_to_all(
        outgoing.reshape(groups, CAPQ * PIECES, piece_cols),
        "dp",
        split_axis=0,
        concat_axis=0,
        tiled=True,
    ).reshape(lines, piece_cols)

    produced = pl.pallas_call(
        ffn_kernel,
        in_specs=[vmem, hbm],
        out_specs=vmem,
        out_shape=pltpu.VMEM((lines, piece_cols), jnp.bfloat16),
        scratch_shapes=[
            pltpu.VMEM((shards, 3, unit, width), jnp.bfloat16),
            pltpu.SemaphoreType.DMA((len(CHUNKS),)),
        ],
        compiler_params=pltpu.CompilerParams(vmem_limit_bytes=40 << 20),
        name="ffn",
    )(in_vmem(incoming), in_hbm(full.reshape(shards, 3, unit, width)))
    returned = lax.all_to_all(
        produced.reshape(groups, CAPQ * PIECES, piece_cols),
        "dp",
        split_axis=0,
        concat_axis=0,
        tiled=True,
    ).reshape(lines, piece_cols)
    finished = pl.pallas_call(
        combine_kernel,
        in_specs=[vmem] * 3,
        out_specs=vmem,
        out_shape=pltpu.VMEM((shards, block, cols), jnp.bfloat16),
        compiler_params=pltpu.CompilerParams(vmem_limit_bytes=8 << 20),
        name="combine",
    )(in_vmem(returned), in_vmem(gate_matrix), in_vmem(mixed))
    result = lax.all_to_all(finished, SPLIT, split_axis=0, concat_axis=0, tiled=True)
    return result.reshape(rows, cols)


def solution(mesh):
    return jax.shard_map(
        local,
        mesh=mesh,
        in_specs=(
            P("dp", ("section", "mp")),
            P("dp", None, ("section", "mp")),
            P("dp", None),
            P(("section", "mp"), None),
            P(),
            P("dp", None, ("section", "mp")),
            P("dp", None, ("section", "mp")),
            P("dp", ("section", "mp"), None),
            P("dp", None, None),
            P("dp", None, None),
            P(),
            P(),
            P("dp", None),
            P("dp", None),
        ),
        out_specs=P("dp", ("section", "mp")),
        check_vma=False,
    )
```

```python
import math

import jax
import jax.numpy as jnp
from jax import lax
from jax.experimental import pallas as pl
from jax.experimental.pallas import tpu as pltpu
from jax.sharding import PartitionSpec as P

HEAD_DIM = 128
LANES = 128
TOPK = 4
PREF = 64
BLK = 8
OWN_CAP = 3
CAPQ = 2
PIECES = 4
CHUNKS = (4, 4)
DOWN_PARTS = 2
SPLIT = ("section", "mp")


def nt_dot(a, b):
    return lax.dot_general(a, b, (((1,), (1,)), ((), ())), preferred_element_type=jnp.float32)


def attend_kernel(
    qkv_ref, prefix_ref, key_seg_ref, seg_row_ref, seg_col_ref, weight_ref, keep_ref, send_ref, rows_ref
):
    rows = qkv_ref.shape[0]
    query = qkv_ref[:, :HEAD_DIM]
    scale = 1.0 / math.sqrt(HEAD_DIM)
    old = nt_dot(query, prefix_ref[:, :HEAD_DIM]) * scale
    new = nt_dot(query, qkv_ref[:, HEAD_DIM : 2 * HEAD_DIM]) * scale
    seg = seg_col_ref[...]
    earlier = lax.broadcasted_iota(jnp.int32, (rows, rows), 1) <= lax.broadcasted_iota(
        jnp.int32, (rows, rows), 0
    )
    old = jnp.where(key_seg_ref[...] == seg, old, -jnp.inf)
    new = jnp.where((seg_row_ref[...] == seg) & earlier, new, -jnp.inf)
    top = jnp.maximum(
        jnp.max(old, axis=1, keepdims=True), jnp.max(new, axis=1, keepdims=True)
    )
    old = jnp.exp(old - top)
    new = jnp.exp(new - top)
    total = jnp.sum(old, axis=1, keepdims=True) + jnp.sum(new, axis=1, keepdims=True)
    old = (old / total).astype(jnp.bfloat16)
    new = (new / total).astype(jnp.bfloat16)
    attended = jnp.dot(
        old, prefix_ref[:, HEAD_DIM:], preferred_element_type=jnp.float32
    ) + jnp.dot(new, qkv_ref[:, 2 * HEAD_DIM :], preferred_element_type=jnp.float32)
    rows_ref[...] = attended.astype(jnp.bfloat16)
    half = keep_ref.shape[0]
    core = lax.axis_index("section")
    for ref, side in ((keep_ref, core), (send_ref, 1 - core)):
        part = rows_ref[pl.ds(pl.multiple_of(side * half, half), half), :]
        ref[...] = jnp.dot(
            part, weight_ref[...], preferred_element_type=jnp.float32
        ).astype(ref.dtype)


def add_kernel(a_ref, b_ref, out_ref):
    out_ref[...] = (a_ref[...] + b_ref[...].astype(jnp.float32)).astype(out_ref.dtype)


def in_vmem(x):
    return pltpu.with_memory_space_constraint(x, pltpu.VMEM)


def in_hbm(x):
    return pltpu.with_memory_space_constraint(x, pltpu.HBM)


def fetch_kernel(*refs):
    count = len(refs) // 2
    sems = refs[-1]
    copies = [
        pltpu.make_async_copy(refs[i], refs[count + i], sems.at[i]) for i in range(count)
    ]
    for copy in copies:
        copy.start()
    for copy in copies:
        copy.wait()


def select_kernel(
    owners_hbm,
    slots_hbm,
    cache_hbm,
    gate_hbm,
    up_hbm,
    down_hbm,
    out_hbm,
    pack_hbm,
    owners_ref,
    slots_ref,
    cache_ref,
    cache_wide,
    out_wide,
    out_ref,
    pack_buf,
    table_sems,
    load_sems,
    store_sems,
    out_sems,
):
    unit = gate_hbm.shape[0]
    tables = [
        pltpu.make_async_copy(source, target, table_sems.at[i])
        for i, (source, target) in enumerate(
            ((owners_hbm, owners_ref), (slots_hbm, slots_ref), (cache_hbm, cache_ref))
        )
    ]
    parts = [pl.ds(i * unit, unit) for i in range(3)]
    loads = [
        pltpu.make_async_copy(source, pack_buf.at[part], load_sems.at[i])
        for i, (source, part) in enumerate(zip((gate_hbm, up_hbm, down_hbm), parts))
    ]
    stores = [
        pltpu.make_async_copy(pack_buf.at[part], pack_hbm.at[part], store_sems.at[i])
        for i, part in enumerate(parts)
    ]
    for copy in tables + loads:
        copy.start()
    tables[0].wait()
    owned = owners_ref[:, 0, :] == lax.axis_index("dp")
    groups, entries = owned.shape
    earlier = lax.broadcasted_iota(jnp.int32, (entries, entries), 0) < lax.broadcasted_iota(
        jnp.int32, (entries, entries), 1
    )
    rank = jnp.dot(
        jnp.where(owned, 1.0, 0.0).astype(jnp.bfloat16),
        jnp.where(earlier, 1.0, 0.0).astype(jnp.bfloat16),
        preferred_element_type=jnp.float32,
    )
    tables[1].wait()
    named = slots_ref[:, 0, :]
    held = cache_ref.shape[0] // BLK
    index = lax.broadcasted_iota(jnp.int32, (groups, held), 1)
    picks = []
    for r in range(OWN_CAP):
        slot = jnp.sum(jnp.where(owned & (rank == r), named, 0), axis=1, keepdims=True)
        picks.append(jnp.where(slot == index, 1.0, 0.0).astype(jnp.bfloat16))
    picks = jnp.concatenate(picks, axis=0)
    tables[2].wait()
    halves = cache_wide.shape[0]
    for h in range(halves):
        cache_wide[h] = cache_ref[:, h * LANES : (h + 1) * LANES].astype(jnp.float32)
    for load, store in zip(loads, stores):
        load.wait()
        store.start()
    outs = []
    for h in range(halves):
        for b in range(BLK):
            part = cache_wide[h, pl.ds(b, held, stride=BLK), :].astype(jnp.bfloat16)
            chosen = jnp.dot(picks, part, preferred_element_type=jnp.float32)
            for r in range(OWN_CAP):
                out_wide[h, pl.ds(r * BLK + b, groups, stride=OWN_CAP * BLK), :] = chosen[
                    r * groups : (r + 1) * groups
                ]
        out_ref[h] = out_wide[h].astype(jnp.bfloat16)
        outs.append(
            pltpu.make_async_copy(
                out_ref.at[h], out_hbm.at[:, pl.ds(h * LANES, LANES)], out_sems.at[h]
            )
        )
        outs[-1].start()
    for copy in outs + stores:
        copy.wait()


def norm_kernel(parts_ref, residual_ref, gain_ref, pick_ref, mixed_ref, out_ref):
    mixed = residual_ref[...].astype(jnp.float32)
    projected = parts_ref[0].astype(jnp.float32)
    for i in range(1, parts_ref.shape[0]):
        projected = projected + parts_ref[i].astype(jnp.float32)
    mixed = mixed + projected
    mixed_ref[...] = mixed
    square = jnp.mean(mixed * mixed, axis=1, keepdims=True)
    normed = (mixed * lax.rsqrt(square + 1e-06) * gain_ref[...]).astype(jnp.bfloat16)
    out_ref[...] = jnp.dot(
        pick_ref[...], stack_pieces(normed), preferred_element_type=jnp.float32
    ).astype(jnp.bfloat16)


def stack_pieces(x):
    cols = x.shape[1] // PIECES
    return jnp.concatenate([x[:, i * cols : (i + 1) * cols] for i in range(PIECES)], axis=0)


def join_pieces(x):
    rows = x.shape[0] // PIECES
    return jnp.concatenate([x[i * rows : (i + 1) * rows] for i in range(PIECES)], axis=1)


def ffn_kernel(x_ref, weight_hbm, out_ref, weight_ref, down_ref, hidden_ref, sems, down_sems):
    shards, _, unit, width = weight_ref.shape
    ends = [sum(CHUNKS[: i + 1]) for i in range(len(CHUNKS))]
    spans = [(end - size, size) for end, size in zip(ends, CHUNKS)]
    assert ends[-1] == shards
    loads = [
        pltpu.make_async_copy(
            weight_hbm.at[pl.ds(first, size), pl.ds(0, 2)],
            weight_ref.at[pl.ds(first, size)],
            sems.at[i],
        )
        for i, (first, size) in enumerate(spans)
    ]
    parts = down_ref.shape[0]
    cols = width // parts
    down_loads = [
        pltpu.make_async_copy(
            weight_hbm.at[:, 2, :, pl.ds(i * cols, cols)], down_ref.at[i], down_sems.at[i]
        )
        for i in range(parts)
    ]
    for load in loads + down_loads:
        load.start()
    total = x_ref.shape[0]
    rows = total // PIECES
    near = lax.broadcasted_iota(jnp.int32, (total, total), 0)
    far = lax.broadcasted_iota(jnp.int32, (total, total), 1)
    to_rows = jnp.where(far == (near % rows) * PIECES + near // rows, 1.0, 0.0).astype(jnp.bfloat16)
    to_pieces = jnp.where(near == (far % rows) * PIECES + far // rows, 1.0, 0.0).astype(
        jnp.bfloat16
    )
    x = join_pieces(
        jnp.dot(to_rows, x_ref[...], preferred_element_type=jnp.float32).astype(jnp.bfloat16)
    )
    for load, (first, size) in zip(loads, spans):
        load.wait()
        gate, up = (
            weight_ref[first : first + size, j].reshape(size * unit, width) for j in range(2)
        )
        gate = nt_dot(x, gate)
        hidden_ref[:, first * unit : (first + size) * unit] = (
            gate / (1.0 + jnp.exp(-gate)) * nt_dot(x, up)
        ).astype(jnp.bfloat16)
    result = []
    for i, load in enumerate(down_loads):
        load.wait()
        down = down_ref[i].reshape(shards * unit, cols)
        result.append(
            jnp.dot(hidden_ref[...], down, preferred_element_type=jnp.float32).astype(jnp.bfloat16)
        )
    out_ref[...] = jnp.dot(
        to_pieces,
        stack_pieces(jnp.concatenate(result, axis=1)),
        preferred_element_type=jnp.float32,
    ).astype(jnp.bfloat16)


def combine_kernel(rows_ref, gate_ref, mixed_ref, out_ref):
    gate = gate_ref[...]
    high = gate.astype(jnp.bfloat16)
    low = (gate - high.astype(jnp.float32)).astype(jnp.bfloat16)
    rows = rows_ref[...]
    total = jnp.dot(high, rows, preferred_element_type=jnp.float32)
    total = total + jnp.dot(low, rows, preferred_element_type=jnp.float32)
    total = (join_pieces(total) + mixed_ref[...]).astype(jnp.bfloat16)
    cols = out_ref.shape[2]
    for i in range(out_ref.shape[0]):
        out_ref[i] = total[:, i * cols : (i + 1) * cols]


def local(
    qkv,
    kv_cache,
    residual,
    out_weight,
    moe_gain,
    w_gate,
    w_up,
    w_down,
    seg_ids,
    prefix_blocks,
    owners,
    slot_ids,
    expert_ids,
    gate_weights,
):
    groups = lax.axis_size("dp")
    shards = lax.axis_size("section") * lax.axis_size("mp")
    group = lax.axis_index("dp")
    shard = lax.axis_index("section") * lax.axis_size("mp") + lax.axis_index("mp")
    rows = seg_ids.shape[2]
    block = rows // shards
    width = residual.shape[1]
    cols = width // shards
    slots = groups * CAPQ

    vmem = pl.BlockSpec(memory_space=pltpu.VMEM)
    hbm = pl.BlockSpec(memory_space=pltpu.HBM)
    table = owners[:, 0, :, 0]
    unit = w_down.shape[1]
    cache_cols = kv_cache.shape[2]
    cache_rows = kv_cache.shape[0] * BLK
    sent_rows = groups * OWN_CAP * BLK
    chosen, packed = pl.pallas_call(
        select_kernel,
        in_specs=[hbm] * 6,
        out_specs=(hbm, hbm),
        out_shape=(
            pltpu.HBM((sent_rows, cache_cols), jnp.bfloat16),
            pltpu.HBM((3 * unit, width), jnp.bfloat16),
        ),
        scratch_shapes=[
            pltpu.VMEM((groups, 1, PREF), jnp.int32),
            pltpu.VMEM((groups, 1, PREF), jnp.int32),
            pltpu.VMEM((cache_rows, cache_cols), jnp.bfloat16),
            pltpu.VMEM((cache_cols // LANES, cache_rows, LANES), jnp.float32),
            pltpu.VMEM((cache_cols // LANES, sent_rows, LANES), jnp.float32),
            pltpu.VMEM((cache_cols // LANES, sent_rows, LANES), jnp.bfloat16),
            pltpu.VMEM((3 * unit, width), jnp.bfloat16),
            pltpu.SemaphoreType.DMA((3,)),
            pltpu.SemaphoreType.DMA((3,)),
            pltpu.SemaphoreType.DMA((3,)),
            pltpu.SemaphoreType.DMA((cache_cols // LANES,)),
        ],
        compiler_params=pltpu.CompilerParams(vmem_limit_bytes=12 << 20),
        name="select",
    )(
        in_hbm(owners[:, :, :, 0]),
        in_hbm(slot_ids),
        in_hbm(kv_cache.reshape(cache_rows, cache_cols)),
        in_hbm(w_gate[0].T),
        in_hbm(w_up[0].T),
        in_hbm(w_down[0]),
    )
    arrived = lax.all_to_all(
        chosen.reshape(groups, OWN_CAP, BLK, cache_cols),
        "dp",
        split_axis=0,
        concat_axis=0,
        tiled=True,
    )
    full = lax.all_gather(packed, SPLIT, axis=0, tiled=True)

    mine = lax.dynamic_index_in_dim(table, group, 0, keepdims=False)
    index = jnp.arange(PREF, dtype=jnp.int32)
    before = (mine[None, :] == mine[:, None]) & (index[None, :] < index[:, None])
    place = mine * OWN_CAP + jnp.sum(before.astype(jnp.int32), axis=1)
    ends = jnp.cumsum(prefix_blocks[0, 0])
    block_seg = jnp.sum((ends[None, :] <= index[:, None]).astype(jnp.int32), axis=1)
    key_slot = jnp.arange(groups * OWN_CAP * BLK, dtype=jnp.int32) // BLK
    key_seg = (
        jnp.sum(jnp.where(place[:, None] == key_slot[None, :], block_seg[:, None] + 1, 0), axis=0)
        - 1
    )[None, :]
    segments = seg_ids[0, 0]

    first = shard * block
    ids = lax.dynamic_slice_in_dim(expert_ids, first, block, 0)
    gates = lax.dynamic_slice_in_dim(gate_weights, first, block, 0)
    flat = ids.reshape(-1)
    pair = jnp.arange(block * TOPK, dtype=jnp.int32)
    same = (flat[None, :] == flat[:, None]) & (pair[None, :] < pair[:, None])
    slot = (flat * CAPQ + jnp.sum(same.astype(jnp.int32), axis=1)).reshape(block, TOPK)
    slot_index = jnp.arange(slots, dtype=jnp.int32)
    line = jnp.arange(slots * PIECES, dtype=jnp.int32)
    piece = jnp.arange(PIECES, dtype=jnp.int32)
    hit = slot[:, :, None] == line[None, None, :] // PIECES
    mine_of_piece = (line[None, :] % PIECES == piece[:, None])[:, None, :]
    gate_matrix = jnp.where(
        mine_of_piece, jnp.sum(jnp.where(hit, gates[:, :, None], 0.0), axis=1)[None], 0.0
    ).reshape(PIECES * block, -1)
    pick_matrix = (
        (mine_of_piece & jnp.any(hit, axis=1)[None]).reshape(PIECES * block, -1).T
    ).astype(jnp.bfloat16)
    my_residual = lax.dynamic_slice_in_dim(residual, first, block, 0)

    near = (qkv, out_weight, moe_gain[None, :])
    near = pl.pallas_call(
        fetch_kernel,
        in_specs=[hbm] * len(near),
        out_specs=(vmem,) * len(near),
        out_shape=tuple(pltpu.VMEM(x.shape, x.dtype) for x in near),
        scratch_shapes=[pltpu.SemaphoreType.DMA((len(near),))],
        compiler_params=pltpu.CompilerParams(vmem_limit_bytes=1 << 20),
        name="fetch",
    )(*[in_hbm(x) for x in near])
    arrived, near, pick_matrix, gate_matrix, my_residual = lax.optimization_barrier(
        (arrived, near, pick_matrix, gate_matrix, my_residual)
    )
    near_qkv, near_weight, near_gain = near
    lines = slots * PIECES
    piece_cols = width // PIECES
    half = rows // lax.axis_size("section")
    kept, sent = pl.pallas_call(
        attend_kernel,
        in_specs=[vmem] * 6,
        out_specs=(vmem, vmem),
        out_shape=(
            pltpu.VMEM((half, width), jnp.float32),
            pltpu.VMEM((half, width), jnp.bfloat16),
        ),
        scratch_shapes=[pltpu.VMEM((rows, HEAD_DIM), jnp.bfloat16)],
        compiler_params=pltpu.CompilerParams(vmem_limit_bytes=16 << 20),
        name="attend",
    )(
        in_vmem(near_qkv),
        in_vmem(arrived.reshape(-1, kv_cache.shape[2])),
        in_vmem(key_seg),
        in_hbm(segments[None, :]),
        in_vmem(segments[:, None]),
        in_vmem(near_weight),
    )
    received = lax.ppermute(sent, "section", [(0, 1), (1, 0)])
    projected = pl.pallas_call(
        add_kernel,
        in_specs=[vmem, vmem],
        out_specs=vmem,
        out_shape=pltpu.VMEM((half, width), jnp.bfloat16),
        compiler_params=pltpu.CompilerParams(vmem_limit_bytes=4 << 20),
        name="add",
    )(in_vmem(kept), in_vmem(received))
    chips = lax.axis_size("mp")
    parts = lax.all_to_all(
        projected.reshape(chips, block, width), "mp", split_axis=0, concat_axis=0, tiled=True
    )
    mixed, outgoing = pl.pallas_call(
        norm_kernel,
        in_specs=[vmem] * 4,
        out_specs=(vmem, vmem),
        out_shape=(
            pltpu.VMEM((block, width), jnp.float32),
            pltpu.VMEM((lines, piece_cols), jnp.bfloat16),
        ),
        compiler_params=pltpu.CompilerParams(vmem_limit_bytes=8 << 20),
        name="norm",
    )(in_vmem(parts), in_vmem(my_residual), in_vmem(near_gain), in_vmem(pick_matrix))
    incoming = lax.all_to_all(
        outgoing.reshape(groups, CAPQ * PIECES, piece_cols),
        "dp",
        split_axis=0,
        concat_axis=0,
        tiled=True,
    ).reshape(lines, piece_cols)

    produced = pl.pallas_call(
        ffn_kernel,
        in_specs=[vmem, hbm],
        out_specs=vmem,
        out_shape=pltpu.VMEM((lines, piece_cols), jnp.bfloat16),
        scratch_shapes=[
            pltpu.VMEM((shards, 2, unit, width), jnp.bfloat16),
            pltpu.VMEM((DOWN_PARTS, shards, unit, width // DOWN_PARTS), jnp.bfloat16),
            pltpu.VMEM((slots, shards * unit), jnp.bfloat16),
            pltpu.SemaphoreType.DMA((len(CHUNKS),)),
            pltpu.SemaphoreType.DMA((DOWN_PARTS,)),
        ],
        compiler_params=pltpu.CompilerParams(vmem_limit_bytes=40 << 20),
        name="ffn",
    )(in_vmem(incoming), in_hbm(full.reshape(shards, 3, unit, width)))
    returned = lax.all_to_all(
        produced.reshape(groups, CAPQ * PIECES, piece_cols),
        "dp",
        split_axis=0,
        concat_axis=0,
        tiled=True,
    ).reshape(lines, piece_cols)
    finished = pl.pallas_call(
        combine_kernel,
        in_specs=[vmem] * 3,
        out_specs=vmem,
        out_shape=pltpu.VMEM((shards, block, cols), jnp.bfloat16),
        compiler_params=pltpu.CompilerParams(vmem_limit_bytes=8 << 20),
        name="combine",
    )(in_vmem(returned), in_vmem(gate_matrix), in_vmem(mixed))
    result = lax.all_to_all(finished, SPLIT, split_axis=0, concat_axis=0, tiled=True)
    return result.reshape(rows, cols)


def solution(mesh):
    return jax.shard_map(
        local,
        mesh=mesh,
        in_specs=(
            P("dp", ("section", "mp")),
            P("dp", None, ("section", "mp")),
            P("dp", None),
            P(("section", "mp"), None),
            P(),
            P("dp", None, ("section", "mp")),
            P("dp", None, ("section", "mp")),
            P("dp", ("section", "mp"), None),
            P("dp", None, None),
            P("dp", None, None),
            P(),
            P(),
            P("dp", None),
            P("dp", None),
        ),
        out_specs=P("dp", ("section", "mp")),
        check_vma=False,
    )
```

```python
import math

import jax
import jax.numpy as jnp
from jax import lax
from jax.experimental import pallas as pl
from jax.experimental.pallas import tpu as pltpu
from jax.sharding import PartitionSpec as P

HEAD_DIM = 128
LANES = 128
TOPK = 4
PREF = 64
BLK = 8
OWN_CAP = 3
CAPQ = 2
PIECES = 4
CHUNKS = (4, 4)
DOWN_PARTS = 2
SPLIT = ("section", "mp")


def nt_dot(a, b):
    return lax.dot_general(a, b, (((1,), (1,)), ((), ())), preferred_element_type=jnp.float32)


def attend_kernel(
    qkv_ref, prefix_ref, key_seg_ref, seg_row_ref, seg_col_ref, weight_ref, keep_ref, send_ref, rows_ref
):
    rows = qkv_ref.shape[0]
    query = qkv_ref[:, :HEAD_DIM]
    scale = 1.0 / math.sqrt(HEAD_DIM)
    old = nt_dot(query, prefix_ref[:, :HEAD_DIM]) * scale
    new = nt_dot(query, qkv_ref[:, HEAD_DIM : 2 * HEAD_DIM]) * scale
    seg = seg_col_ref[...]
    earlier = lax.broadcasted_iota(jnp.int32, (rows, rows), 1) <= lax.broadcasted_iota(
        jnp.int32, (rows, rows), 0
    )
    old = jnp.where(key_seg_ref[...] == seg, old, -jnp.inf)
    new = jnp.where((seg_row_ref[...] == seg) & earlier, new, -jnp.inf)
    top = jnp.maximum(
        jnp.max(old, axis=1, keepdims=True), jnp.max(new, axis=1, keepdims=True)
    )
    old = jnp.exp(old - top)
    new = jnp.exp(new - top)
    total = jnp.sum(old, axis=1, keepdims=True) + jnp.sum(new, axis=1, keepdims=True)
    old = old.astype(jnp.bfloat16)
    new = new.astype(jnp.bfloat16)
    attended = jnp.dot(
        old, prefix_ref[:, HEAD_DIM:], preferred_element_type=jnp.float32
    ) + jnp.dot(new, qkv_ref[:, 2 * HEAD_DIM :], preferred_element_type=jnp.float32)
    rows_ref[...] = (attended / total).astype(jnp.bfloat16)
    half = keep_ref.shape[0]
    core = lax.axis_index("section")
    for ref, side in ((keep_ref, core), (send_ref, 1 - core)):
        part = rows_ref[pl.ds(pl.multiple_of(side * half, half), half), :]
        ref[...] = jnp.dot(
            part, weight_ref[...], preferred_element_type=jnp.float32
        ).astype(ref.dtype)


def add_kernel(a_ref, b_ref, out_ref):
    out_ref[...] = (a_ref[...] + b_ref[...].astype(jnp.float32)).astype(out_ref.dtype)


def in_vmem(x):
    return pltpu.with_memory_space_constraint(x, pltpu.VMEM)


def in_hbm(x):
    return pltpu.with_memory_space_constraint(x, pltpu.HBM)


def fetch_kernel(*refs):
    count = len(refs) // 2
    sems = refs[-1]
    copies = [
        pltpu.make_async_copy(refs[i], refs[count + i], sems.at[i]) for i in range(count)
    ]
    for copy in copies:
        copy.start()
    for copy in copies:
        copy.wait()


def select_kernel(
    owners_hbm,
    slots_hbm,
    cache_hbm,
    gate_hbm,
    up_hbm,
    down_hbm,
    out_hbm,
    pack_hbm,
    owners_ref,
    slots_ref,
    cache_ref,
    cache_wide,
    out_wide,
    out_ref,
    pack_buf,
    table_sems,
    load_sems,
    store_sems,
    out_sems,
):
    unit = gate_hbm.shape[0]
    tables = [
        pltpu.make_async_copy(source, target, table_sems.at[i])
        for i, (source, target) in enumerate(
            ((owners_hbm, owners_ref), (slots_hbm, slots_ref), (cache_hbm, cache_ref))
        )
    ]
    parts = [pl.ds(i * unit, unit) for i in range(3)]
    loads = [
        pltpu.make_async_copy(source, pack_buf.at[part], load_sems.at[i])
        for i, (source, part) in enumerate(zip((gate_hbm, up_hbm, down_hbm), parts))
    ]
    stores = [
        pltpu.make_async_copy(pack_buf.at[part], pack_hbm.at[part], store_sems.at[i])
        for i, part in enumerate(parts)
    ]
    for copy in tables + loads:
        copy.start()
    tables[0].wait()
    owned = owners_ref[:, 0, :] == lax.axis_index("dp")
    groups, entries = owned.shape
    earlier = lax.broadcasted_iota(jnp.int32, (entries, entries), 0) < lax.broadcasted_iota(
        jnp.int32, (entries, entries), 1
    )
    rank = jnp.dot(
        jnp.where(owned, 1.0, 0.0).astype(jnp.bfloat16),
        jnp.where(earlier, 1.0, 0.0).astype(jnp.bfloat16),
        preferred_element_type=jnp.float32,
    )
    tables[1].wait()
    named = slots_ref[:, 0, :]
    held = cache_ref.shape[0] // BLK
    index = lax.broadcasted_iota(jnp.int32, (groups, held), 1)
    picks = []
    for r in range(OWN_CAP):
        slot = jnp.sum(jnp.where(owned & (rank == r), named, 0), axis=1, keepdims=True)
        picks.append(jnp.where(slot == index, 1.0, 0.0).astype(jnp.bfloat16))
    picks = jnp.concatenate(picks, axis=0)
    tables[2].wait()
    halves = cache_wide.shape[0]
    for h in range(halves):
        cache_wide[h] = cache_ref[:, h * LANES : (h + 1) * LANES].astype(jnp.float32)
    for load, store in zip(loads, stores):
        load.wait()
        store.start()
    outs = []
    for h in range(halves):
        for b in range(BLK):
            part = cache_wide[h, pl.ds(b, held, stride=BLK), :].astype(jnp.bfloat16)
            chosen = jnp.dot(picks, part, preferred_element_type=jnp.float32)
            for r in range(OWN_CAP):
                out_wide[h, pl.ds(r * BLK + b, groups, stride=OWN_CAP * BLK), :] = chosen[
                    r * groups : (r + 1) * groups
                ]
        out_ref[h] = out_wide[h].astype(jnp.bfloat16)
        outs.append(
            pltpu.make_async_copy(
                out_ref.at[h], out_hbm.at[:, pl.ds(h * LANES, LANES)], out_sems.at[h]
            )
        )
        outs[-1].start()
    for copy in outs + stores:
        copy.wait()


def norm_kernel(parts_ref, residual_ref, gain_ref, pick_ref, mixed_ref, out_ref):
    mixed = residual_ref[...].astype(jnp.float32)
    projected = parts_ref[0].astype(jnp.float32)
    for i in range(1, parts_ref.shape[0]):
        projected = projected + parts_ref[i].astype(jnp.float32)
    mixed = mixed + projected
    mixed_ref[...] = mixed
    square = jnp.mean(mixed * mixed, axis=1, keepdims=True)
    normed = (mixed * lax.rsqrt(square + 1e-06) * gain_ref[...]).astype(jnp.bfloat16)
    out_ref[...] = jnp.dot(
        pick_ref[...], stack_pieces(normed), preferred_element_type=jnp.float32
    ).astype(jnp.bfloat16)


def stack_pieces(x):
    cols = x.shape[1] // PIECES
    return jnp.concatenate([x[:, i * cols : (i + 1) * cols] for i in range(PIECES)], axis=0)


def join_pieces(x):
    rows = x.shape[0] // PIECES
    return jnp.concatenate([x[i * rows : (i + 1) * rows] for i in range(PIECES)], axis=1)


def ffn_kernel(x_ref, weight_hbm, out_ref, weight_ref, down_ref, hidden_ref, sems, down_sems):
    shards, _, unit, width = weight_ref.shape
    ends = [sum(CHUNKS[: i + 1]) for i in range(len(CHUNKS))]
    spans = [(end - size, size) for end, size in zip(ends, CHUNKS)]
    assert ends[-1] == shards
    loads = [
        pltpu.make_async_copy(
            weight_hbm.at[pl.ds(first, size), pl.ds(0, 2)],
            weight_ref.at[pl.ds(first, size)],
            sems.at[i],
        )
        for i, (first, size) in enumerate(spans)
    ]
    parts = down_ref.shape[0]
    cols = width // parts
    down_loads = [
        pltpu.make_async_copy(
            weight_hbm.at[:, 2, :, pl.ds(i * cols, cols)], down_ref.at[i], down_sems.at[i]
        )
        for i in range(parts)
    ]
    for load in loads + down_loads:
        load.start()
    total = x_ref.shape[0]
    rows = total // PIECES
    near = lax.broadcasted_iota(jnp.int32, (total, total), 0)
    far = lax.broadcasted_iota(jnp.int32, (total, total), 1)
    to_rows = jnp.where(far == (near % rows) * PIECES + near // rows, 1.0, 0.0).astype(jnp.bfloat16)
    to_pieces = jnp.where(near == (far % rows) * PIECES + far // rows, 1.0, 0.0).astype(
        jnp.bfloat16
    )
    x = join_pieces(
        jnp.dot(to_rows, x_ref[...], preferred_element_type=jnp.float32).astype(jnp.bfloat16)
    )
    for load, (first, size) in zip(loads, spans):
        load.wait()
        gate, up = (
            weight_ref[first : first + size, j].reshape(size * unit, width) for j in range(2)
        )
        gate = nt_dot(x, gate)
        hidden_ref[:, first * unit : (first + size) * unit] = (
            gate / (1.0 + jnp.exp(-gate)) * nt_dot(x, up)
        ).astype(jnp.bfloat16)
    result = []
    for i, load in enumerate(down_loads):
        load.wait()
        down = down_ref[i].reshape(shards * unit, cols)
        result.append(
            jnp.dot(hidden_ref[...], down, preferred_element_type=jnp.float32).astype(jnp.bfloat16)
        )
    out_ref[...] = jnp.dot(
        to_pieces,
        stack_pieces(jnp.concatenate(result, axis=1)),
        preferred_element_type=jnp.float32,
    ).astype(jnp.bfloat16)


def combine_kernel(rows_ref, gate_ref, mixed_ref, out_ref):
    gate = gate_ref[...]
    high = gate.astype(jnp.bfloat16)
    low = (gate - high.astype(jnp.float32)).astype(jnp.bfloat16)
    rows = rows_ref[...]
    total = jnp.dot(high, rows, preferred_element_type=jnp.float32)
    total = total + jnp.dot(low, rows, preferred_element_type=jnp.float32)
    total = (join_pieces(total) + mixed_ref[...]).astype(jnp.bfloat16)
    cols = out_ref.shape[2]
    for i in range(out_ref.shape[0]):
        out_ref[i] = total[:, i * cols : (i + 1) * cols]


def local(
    qkv,
    kv_cache,
    residual,
    out_weight,
    moe_gain,
    w_gate,
    w_up,
    w_down,
    seg_ids,
    prefix_blocks,
    owners,
    slot_ids,
    expert_ids,
    gate_weights,
):
    groups = lax.axis_size("dp")
    shards = lax.axis_size("section") * lax.axis_size("mp")
    group = lax.axis_index("dp")
    shard = lax.axis_index("section") * lax.axis_size("mp") + lax.axis_index("mp")
    rows = seg_ids.shape[2]
    block = rows // shards
    width = residual.shape[1]
    cols = width // shards
    slots = groups * CAPQ

    vmem = pl.BlockSpec(memory_space=pltpu.VMEM)
    hbm = pl.BlockSpec(memory_space=pltpu.HBM)
    table = owners[:, 0, :, 0]
    unit = w_down.shape[1]
    cache_cols = kv_cache.shape[2]
    cache_rows = kv_cache.shape[0] * BLK
    sent_rows = groups * OWN_CAP * BLK
    chosen, packed = pl.pallas_call(
        select_kernel,
        in_specs=[hbm] * 6,
        out_specs=(hbm, hbm),
        out_shape=(
            pltpu.HBM((sent_rows, cache_cols), jnp.bfloat16),
            pltpu.HBM((3 * unit, width), jnp.bfloat16),
        ),
        scratch_shapes=[
            pltpu.VMEM((groups, 1, PREF), jnp.int32),
            pltpu.VMEM((groups, 1, PREF), jnp.int32),
            pltpu.VMEM((cache_rows, cache_cols), jnp.bfloat16),
            pltpu.VMEM((cache_cols // LANES, cache_rows, LANES), jnp.float32),
            pltpu.VMEM((cache_cols // LANES, sent_rows, LANES), jnp.float32),
            pltpu.VMEM((cache_cols // LANES, sent_rows, LANES), jnp.bfloat16),
            pltpu.VMEM((3 * unit, width), jnp.bfloat16),
            pltpu.SemaphoreType.DMA((3,)),
            pltpu.SemaphoreType.DMA((3,)),
            pltpu.SemaphoreType.DMA((3,)),
            pltpu.SemaphoreType.DMA((cache_cols // LANES,)),
        ],
        compiler_params=pltpu.CompilerParams(vmem_limit_bytes=12 << 20),
        name="select",
    )(
        in_hbm(owners[:, :, :, 0]),
        in_hbm(slot_ids),
        in_hbm(kv_cache.reshape(cache_rows, cache_cols)),
        in_hbm(w_gate[0].T),
        in_hbm(w_up[0].T),
        in_hbm(w_down[0]),
    )
    arrived = lax.all_to_all(
        chosen.reshape(groups, OWN_CAP, BLK, cache_cols),
        "dp",
        split_axis=0,
        concat_axis=0,
        tiled=True,
    )
    full = lax.all_gather(packed, SPLIT, axis=0, tiled=True)

    mine = lax.dynamic_index_in_dim(table, group, 0, keepdims=False)
    index = jnp.arange(PREF, dtype=jnp.int32)
    before = (mine[None, :] == mine[:, None]) & (index[None, :] < index[:, None])
    place = mine * OWN_CAP + jnp.sum(before.astype(jnp.int32), axis=1)
    ends = jnp.cumsum(prefix_blocks[0, 0])
    block_seg = jnp.sum((ends[None, :] <= index[:, None]).astype(jnp.int32), axis=1)
    key_slot = jnp.arange(groups * OWN_CAP * BLK, dtype=jnp.int32) // BLK
    key_seg = (
        jnp.sum(jnp.where(place[:, None] == key_slot[None, :], block_seg[:, None] + 1, 0), axis=0)
        - 1
    )[None, :]
    segments = seg_ids[0, 0]

    first = shard * block
    ids = lax.dynamic_slice_in_dim(expert_ids, first, block, 0)
    gates = lax.dynamic_slice_in_dim(gate_weights, first, block, 0)
    flat = ids.reshape(-1)
    pair = jnp.arange(block * TOPK, dtype=jnp.int32)
    same = (flat[None, :] == flat[:, None]) & (pair[None, :] < pair[:, None])
    slot = (flat * CAPQ + jnp.sum(same.astype(jnp.int32), axis=1)).reshape(block, TOPK)
    slot_index = jnp.arange(slots, dtype=jnp.int32)
    line = jnp.arange(slots * PIECES, dtype=jnp.int32)
    piece = jnp.arange(PIECES, dtype=jnp.int32)
    hit = slot[:, :, None] == line[None, None, :] // PIECES
    mine_of_piece = (line[None, :] % PIECES == piece[:, None])[:, None, :]
    gate_matrix = jnp.where(
        mine_of_piece, jnp.sum(jnp.where(hit, gates[:, :, None], 0.0), axis=1)[None], 0.0
    ).reshape(PIECES * block, -1)
    pick_matrix = (
        (mine_of_piece & jnp.any(hit, axis=1)[None]).reshape(PIECES * block, -1).T
    ).astype(jnp.bfloat16)
    my_residual = lax.dynamic_slice_in_dim(residual, first, block, 0)

    near = (qkv, out_weight, moe_gain[None, :])
    near = pl.pallas_call(
        fetch_kernel,
        in_specs=[hbm] * len(near),
        out_specs=(vmem,) * len(near),
        out_shape=tuple(pltpu.VMEM(x.shape, x.dtype) for x in near),
        scratch_shapes=[pltpu.SemaphoreType.DMA((len(near),))],
        compiler_params=pltpu.CompilerParams(vmem_limit_bytes=1 << 20),
        name="fetch",
    )(*[in_hbm(x) for x in near])
    arrived, near, pick_matrix, gate_matrix, my_residual = lax.optimization_barrier(
        (arrived, near, pick_matrix, gate_matrix, my_residual)
    )
    near_qkv, near_weight, near_gain = near
    lines = slots * PIECES
    piece_cols = width // PIECES
    half = rows // lax.axis_size("section")
    kept, sent = pl.pallas_call(
        attend_kernel,
        in_specs=[vmem] * 6,
        out_specs=(vmem, vmem),
        out_shape=(
            pltpu.VMEM((half, width), jnp.float32),
            pltpu.VMEM((half, width), jnp.bfloat16),
        ),
        scratch_shapes=[pltpu.VMEM((rows, HEAD_DIM), jnp.bfloat16)],
        compiler_params=pltpu.CompilerParams(vmem_limit_bytes=16 << 20),
        name="attend",
    )(
        in_vmem(near_qkv),
        in_vmem(arrived.reshape(-1, kv_cache.shape[2])),
        in_vmem(key_seg),
        in_hbm(segments[None, :]),
        in_vmem(segments[:, None]),
        in_vmem(near_weight),
    )
    received = lax.ppermute(sent, "section", [(0, 1), (1, 0)])
    projected = pl.pallas_call(
        add_kernel,
        in_specs=[vmem, vmem],
        out_specs=vmem,
        out_shape=pltpu.VMEM((half, width), jnp.bfloat16),
        compiler_params=pltpu.CompilerParams(vmem_limit_bytes=4 << 20),
        name="add",
    )(in_vmem(kept), in_vmem(received))
    chips = lax.axis_size("mp")
    parts = lax.all_to_all(
        projected.reshape(chips, block, width), "mp", split_axis=0, concat_axis=0, tiled=True
    )
    mixed, outgoing = pl.pallas_call(
        norm_kernel,
        in_specs=[vmem] * 4,
        out_specs=(vmem, vmem),
        out_shape=(
            pltpu.VMEM((block, width), jnp.float32),
            pltpu.VMEM((lines, piece_cols), jnp.bfloat16),
        ),
        compiler_params=pltpu.CompilerParams(vmem_limit_bytes=8 << 20),
        name="norm",
    )(in_vmem(parts), in_vmem(my_residual), in_vmem(near_gain), in_vmem(pick_matrix))
    incoming = lax.all_to_all(
        outgoing.reshape(groups, CAPQ * PIECES, piece_cols),
        "dp",
        split_axis=0,
        concat_axis=0,
        tiled=True,
    ).reshape(lines, piece_cols)

    produced = pl.pallas_call(
        ffn_kernel,
        in_specs=[vmem, hbm],
        out_specs=vmem,
        out_shape=pltpu.VMEM((lines, piece_cols), jnp.bfloat16),
        scratch_shapes=[
            pltpu.VMEM((shards, 2, unit, width), jnp.bfloat16),
            pltpu.VMEM((DOWN_PARTS, shards, unit, width // DOWN_PARTS), jnp.bfloat16),
            pltpu.VMEM((slots, shards * unit), jnp.bfloat16),
            pltpu.SemaphoreType.DMA((len(CHUNKS),)),
            pltpu.SemaphoreType.DMA((DOWN_PARTS,)),
        ],
        compiler_params=pltpu.CompilerParams(vmem_limit_bytes=40 << 20),
        name="ffn",
    )(in_vmem(incoming), in_hbm(full.reshape(shards, 3, unit, width)))
    returned = lax.all_to_all(
        produced.reshape(groups, CAPQ * PIECES, piece_cols),
        "dp",
        split_axis=0,
        concat_axis=0,
        tiled=True,
    ).reshape(lines, piece_cols)
    finished = pl.pallas_call(
        combine_kernel,
        in_specs=[vmem] * 3,
        out_specs=vmem,
        out_shape=pltpu.VMEM((shards, block, cols), jnp.bfloat16),
        compiler_params=pltpu.CompilerParams(vmem_limit_bytes=8 << 20),
        name="combine",
    )(in_vmem(returned), in_vmem(gate_matrix), in_vmem(mixed))
    result = lax.all_to_all(finished, SPLIT, split_axis=0, concat_axis=0, tiled=True)
    return result.reshape(rows, cols)


def solution(mesh):
    return jax.shard_map(
        local,
        mesh=mesh,
        in_specs=(
            P("dp", ("section", "mp")),
            P("dp", None, ("section", "mp")),
            P("dp", None),
            P(("section", "mp"), None),
            P(),
            P("dp", None, ("section", "mp")),
            P("dp", None, ("section", "mp")),
            P("dp", ("section", "mp"), None),
            P("dp", None, None),
            P("dp", None, None),
            P(),
            P(),
            P("dp", None),
            P("dp", None),
        ),
        out_specs=P("dp", ("section", "mp")),
        check_vma=False,
    )
```
